32 devices in a mesh: groups: 1, expert: 32 (over z, y, x, core).
Axes of the slice: x: 2, y: 2, z: 4, core: 2. Of those that a mesh axis runs over, the one named last changes fastest.
Arguments:
- normed: bfloat16 [256, 7168], P(('groups', 'expert')), may hold values from -6 to 6
- expert_ids: int32 [256, 2], P(('groups', 'expert')), may hold values from 0 to 3, all different within a row; in each aligned block of 8 rows (0 to 7, 8 to 15, ...) at most 5 rows name the same one
- gate_levels: int32 [256, 2], P(('groups', 'expert')), may hold values from 1 to 255
- placement: int32 [32], replicated, may hold values from 0 to 3, as said below
- w_gate: bfloat16 [32, 7168, 256], P('expert'), may hold values from -0.0625 to 0.0625
- w_up: bfloat16 [32, 7168, 256], P('expert'), may hold values from -0.0625 to 0.0625
- w_down: bfloat16 [32, 256, 7168], P('expert'), may hold values from -0.125 to 0.125
- q_latent: bfloat16 [256, 64, 512], P(('groups', 'expert')), may hold values from -48 to 48
- q_rope: bfloat16 [256, 4096], P(('groups', 'expert')), may hold values from -48 to 48
- cache_latent: bfloat16 [256, 64, 512], P(('groups', 'expert')), may hold values from -6 to 6
- cache_rope: bfloat16 [256, 64, 64], P(('groups', 'expert')), may hold values from -6 to 6
- lengths: int32 [256], P(('groups', 'expert')), may hold values from 2 to 64, as said below
Outputs:
- moe_out: bfloat16 [256, 7168], P(('groups', 'expert'))
- attended: bfloat16 [256, 64, 512], P(('groups', 'expert'))
The draws below stay inside these ranges and needn't reach their ends.
Inputs may be any that keep to these rules, and one draw needn't show every extreme that they name: `expert_ids`: within the rows of one device an expert is named at most 5 times. `placement`: each expert is held by exactly 8 devices. `lengths`: some device holds a request of 64 positions.
All inputs are finite; a program needn't handle non-finite values.
Results may differ from the reference program's by a relative error of at most 0.0085.
Values may be sent and summed in bfloat16 or wider, within the bound.
A program may use at most 128 MiB of HBM per device.

```python
import math
import jax
import jax.numpy as jnp
import numpy as np
from jax import lax

D = 7168
FF = 2048
FF_DEV = 256
TOPK = 2
HEADS = 64
LAT = 512
ROPE = 64
ROWS = 8
LMAX = 64
SPLIT = 8
SLICES = 32
EXPERTS = 4
CAP = 5
TOKENS = 256


def attention_draw(key):
    key_lat, key_rope, key_query, key_qrope = jax.random.split(jax.random.fold_in(key, 11), 4)
    cache_lat = jnp.clip(jax.random.normal(key_lat, (TOKENS, LMAX, LAT), jnp.float32), -6.0, 6.0)
    cache_pos = jnp.clip(jax.random.normal(key_rope, (TOKENS, ROPE, LMAX), jnp.float32), -6.0, 6.0)
    query_lat = jnp.clip(jax.random.normal(key_query, (TOKENS, HEADS, LAT), jnp.float32), -6.0, 6.0)
    query_pos = jnp.clip(jax.random.normal(key_qrope, (TOKENS, HEADS, ROPE), jnp.float32), -6.0, 6.0)
    return (query_lat, query_pos.reshape(TOKENS, HEADS * ROPE), cache_lat, cache_pos)


def draw_q_latent(key, part):
    return attention_draw(key)[0].astype(jnp.bfloat16)


def draw_q_rope(key, part):
    return attention_draw(key)[1].astype(jnp.bfloat16)


def draw_cache_latent(key, part):
    return attention_draw(key)[2].astype(jnp.bfloat16)


def draw_cache_rope(key, part):
    return attention_draw(key)[3].astype(jnp.bfloat16)


def draw_placement(key, part):
    order = jax.random.permutation(jax.random.fold_in(key, 5), SLICES)
    return (order // SPLIT).astype(jnp.int32)


def draw_lengths(key, part):
    key_cap, key_long, key_len, key_pick = jax.random.split(jax.random.fold_in(key, 3), 4)
    devices = TOKENS // ROWS
    device_caps = jax.random.randint(key_cap, (devices,), LMAX // 4, LMAX + 1)
    longest = jax.random.randint(key_long, (), 0, devices)
    device_caps = jnp.where(jnp.arange(devices) == longest, LMAX, device_caps)
    drawn_lengths = jax.random.randint(key_len, (devices, ROWS), 2, device_caps[:, None] + 1)
    chosen = jax.random.randint(key_pick, (devices,), 0, ROWS)
    drawn_lengths = jnp.where(jnp.arange(ROWS)[None, :] == chosen[:, None], device_caps[:, None], drawn_lengths)
    return drawn_lengths.reshape(TOKENS).astype(jnp.int32)


def with_ends(values, key, smallest, high):
    extent = values.shape
    spot = [jax.random.randint(jax.random.fold_in(key, axis), (), 0, extent[axis]) for axis in range(len(extent))]
    values = values.at[tuple(spot)].set(smallest)
    longest = extent.index(max(extent))
    spot[longest] = (spot[longest] + 1) % extent[longest]
    return values.at[tuple(spot)].set(high)


def block_levels(key, shape, cuts, low, largest):
    gain, own = 1.0, jax.random.fold_in(key, 6)
    for dim, parts in cuts:
        heights = jnp.exp(jax.random.uniform(jax.random.fold_in(own, dim), (parts,), jnp.float32, low / len(cuts), largest / len(cuts)))
        gain = gain * jnp.repeat(heights, shape[dim] // parts).reshape([-1 if axis == dim else 1 for axis in range(len(shape))])
    return gain


def routed_block(stream_key, own, number, rows, count, top, bound, slope):
    order = jax.random.permutation(stream_key, count)
    packed, usual = load_shares(count, rows * top, bound, slope, True), load_shares(count, rows * top, bound, slope, False)
    places = jnp.arange(count)

    def named(sizes, rotation):
        used = int((sizes > 0).sum())
        fixed = max(1, used // 4)
        shifted = fixed + (places - fixed + rotation * (used - fixed)) % max(1, count - fixed)
        return jnp.zeros((count,), jnp.int32).at[order[jnp.where(places < fixed, places, shifted)]].set(jnp.asarray(sizes, jnp.int32))

    sizes = jnp.where(number % 4 == 0, named(packed, number // 4), named(usual, number - number // 4 - 1))
    mixed = jax.random.permutation(jax.random.fold_in(own, 3), count)
    source_of, taker = mixed[0:count // 2 * 2:2], mixed[1:count // 2 * 2:2]
    slack = jnp.minimum(sizes[source_of] - 1, bound - sizes[taker]) // 2
    slack = jnp.where((source_of == order[0]) | (taker == order[0]) | (sizes[taker] == 0), 0, jnp.maximum(slack, 0))
    shifted = jax.random.randint(jax.random.fold_in(own, 4), (count // 2,), 0, 1 << 20) % (slack + 1)
    sizes = sizes.at[source_of].add(-shifted).at[taker].add(shifted)
    members = jnp.searchsorted(jnp.cumsum(sizes), jnp.arange(rows * top), side="right").astype(jnp.int32)
    grid = members.reshape(top, rows).T
    grid = grid[jax.random.permutation(jax.random.fold_in(own, 1), rows)]
    rotation = jax.random.randint(jax.random.fold_in(own, 2), (rows, 1), 0, top)
    return jnp.take_along_axis(grid, (jnp.arange(top)[None, :] + rotation) % top, axis=1)


def load_shares(amount, total, reach, lean, full):
    weights = [(1 << 20) // math.isqrt(rank ** lean) + 1 for rank in range(1, amount + 1)]
    largest = reach if full else min(reach, max(-(-total // amount), total * weights[0] // sum(weights)))
    least = 1 if total - largest >= amount - 1 else 0
    given, rest = [largest] + [least] * (amount - 1), total - largest - least * (amount - 1)
    while rest > 0:
        movable = [i for i in range(1, amount) if given[i] < largest] or [i for i in range(1, amount) if given[i] < reach]
        whole, remaining = sum([weights[i] for i in movable]), rest
        for i in movable:
            addition = min(reach - given[i], max(1, remaining * weights[i] // whole), rest)
            given[i] = given[i] + addition
            rest = rest - addition
    return np.array(given)


def noise(own_key, extent, scale, most, cuts=(), dtype=jnp.bfloat16):
    entries = scale * jax.random.normal(own_key, extent, jnp.float32)
    if cuts:
        entries = entries * block_levels(own_key, extent, cuts, -0.22, 0.18)
    return jnp.clip(entries, -most, most).astype(dtype)


def setup_inputs(seed: int = 0, part: int = 0) -> dict:
    key_list = jax.random.split(jax.random.key(seed), 13)
    part_keys = jax.random.split(jax.random.fold_in(key_list[12], part), 13)
    normed = noise(part_keys[0], (TOKENS, D), 1.0, 6.0, ((0, 32),))
    expert_ids_keys = jax.random.split(jax.random.fold_in(part_keys[1], 1), TOKENS // ROWS)
    expert_ids_turns = jax.random.permutation(jax.random.fold_in(part_keys[1], 3), TOKENS // ROWS)
    expert_ids = jax.vmap(lambda own, number: routed_block(jax.random.fold_in(part_keys[1], 2), own, number, ROWS, EXPERTS, TOPK, CAP, 2))(expert_ids_keys, expert_ids_turns).reshape((TOKENS, TOPK))
    gate_levels = with_ends(jax.random.randint(part_keys[2], (TOKENS, TOPK), 1, 256), jax.random.fold_in(part_keys[2], 1), 1, 255).astype(jnp.int32)
    placement = draw_placement(jax.random.fold_in(key_list[12], 71), part)
    w_gate = noise(key_list[4], (SLICES, D, FF_DEV), D ** -0.5, 0.0625, ((0, 32),))
    w_up = noise(key_list[5], (SLICES, D, FF_DEV), D ** -0.5, 0.0625, ((0, 32),))
    w_down = noise(key_list[6], (SLICES, FF_DEV, D), FF ** -0.5, 0.125, ((0, 32),))
    q_latent = draw_q_latent(jax.random.fold_in(jax.random.fold_in(key_list[12], part), 71), part)
    q_rope = draw_q_rope(jax.random.fold_in(jax.random.fold_in(key_list[12], part), 71), part)
    cache_latent = draw_cache_latent(jax.random.fold_in(jax.random.fold_in(key_list[12], part), 71), part)
    cache_rope = draw_cache_rope(jax.random.fold_in(jax.random.fold_in(key_list[12], part), 71), part)
    lengths = draw_lengths(jax.random.fold_in(jax.random.fold_in(key_list[12], part), 71), part)
    return dict(normed=normed, expert_ids=expert_ids, gate_levels=gate_levels, placement=placement, w_gate=w_gate, w_up=w_up, w_down=w_down, q_latent=q_latent, q_rope=q_rope, cache_latent=cache_latent, cache_rope=cache_rope, lengths=lengths)


score_scale = 192.0 ** -0.5
route_scale = 2.5


def route_weights(gate_levels):
    levels = gate_levels.astype(jnp.float32)
    return route_scale * levels / jnp.sum(levels, axis=1, keepdims=True)


def reference(normed, expert_ids, gate_levels, placement, w_gate, w_up, w_down, q_latent, q_rope, cache_latent, cache_rope, lengths):
    weights = route_weights(gate_levels)

    def one_slice(running, inputs):
        gate_mat, up_mat, down_mat, expert = inputs
        gate_proj = jnp.dot(normed, gate_mat, preferred_element_type=jnp.float32)
        up_proj = jnp.dot(normed, up_mat, preferred_element_type=jnp.float32)
        hidden = (jax.nn.silu(gate_proj) * up_proj).astype(jnp.bfloat16)
        partial_value = jnp.dot(hidden, down_mat, preferred_element_type=jnp.float32).astype(jnp.bfloat16)
        partial_value = lax.optimization_barrier(partial_value).astype(jnp.float32)
        coefficient = jnp.sum(jnp.where(expert_ids == expert, weights, jnp.zeros_like(weights)), axis=1)
        return running + coefficient[:, None] * partial_value, None

    running, ignored = lax.scan(one_slice, jnp.zeros((TOKENS, D), jnp.float32), (w_gate, w_up, w_down, placement))
    moe_out = running.astype(jnp.bfloat16)

    rope_query = q_rope.reshape(TOKENS, HEADS, ROPE).astype(jnp.float32)
    scores = jnp.einsum('bhc,blc->bhl', q_latent.astype(jnp.float32), cache_latent.astype(jnp.float32))
    scores = scores + jnp.einsum('bhr,brl->bhl', rope_query, cache_rope.astype(jnp.float32))
    scores = scores * score_scale
    visible = jnp.arange(LMAX)[None, None, :] < lengths[:, None, None]
    scores = jnp.where(visible, scores, jnp.full_like(scores, -1e30))
    top_score = jnp.max(scores, axis=-1, keepdims=True)
    exponent = jnp.where(visible, jnp.exp(scores - top_score), jnp.zeros_like(scores))
    probs = (exponent / jnp.sum(exponent, axis=-1, keepdims=True)).astype(jnp.bfloat16)
    attended = jnp.einsum('bhl,blc->bhc', probs.astype(jnp.float32), cache_latent.astype(jnp.float32)).astype(jnp.bfloat16)
    return (moe_out, attended)
```

```python
import functools

import jax
import jax.numpy as jnp
from jax import lax
from jax.experimental import pallas as pl
from jax.experimental.pallas import tpu as pltpu
from jax.sharding import PartitionSpec as P

score_scale = 192.0 ** (-0.5)
route_scale = 2.5
BF, F32 = jnp.bfloat16, jnp.float32
EXTRA = 128
PA, PR = 3, 2
SIDE_A, SIDE_B = range(2)


def chip_grid(n):
    return (4, 2, 2) if n == 32 else (n // 2, 1, 1)


def parts(cols, most):
    return max(p for p in range(1, most + 1) if cols % (128 * p) == 0)


def line_body(
    n,
    normed_ref, ids_ref, lev_ref, len_ref, place_ref, wg_hbm, wu_hbm, wd_hbm,
    ql_hbm, qr_ref, cl_hbm, cr_hbm,
    moe_ref, att_hbm,
    xs, acc, rc, rb, ra, rz, wg, wu, wd, h3, cf, rq, gacc, uacc, ql_ref, cl_ref, cr_ref, att_ref,
    w_sem, in_sem, out_sem, ag_ss, ag_rs, agz_ss, agc_ss, agc_rs, rs_ss, rsz_ss, rsc_ss, rc_s, rb_s, ra_s, rz_s,
):
    Z, Y, X = chip_grid(n)
    plane = Y * X
    planar = plane > 1
    chips = n // 2
    R, D = normed_ref.shape
    F = wg.shape[1]
    top = ids_ref.shape[0]
    me = lax.axis_index("expert")
    c = me % 2
    chip = me // 2
    z = chip // plane
    y = (chip % plane) // X
    x = chip % X
    a = x * (1 - c) + y * c
    b = y * (1 - c) + x * c
    sa = (1 - c) + X * c
    sb = X * (1 - c) + c
    peer_a = me + 2 * (1 - 2 * a) * sa
    peer_b = me + 2 * (1 - 2 * b) * sb
    peer_c = 2 * chip + 1 - c

    def at(zz, aa, bb):
        if planar:
            return zz * plane + aa * sa + bb * sb
        return zz

    barrier = pltpu.get_barrier_semaphore()

    def greet(dev):
        pl.semaphore_signal(barrier, inc=1, device_id={"expert": dev})

    greet(peer_c)
    if planar:
        greet(peer_a)
        greet(peer_b)
    for d in range(1, Z):
        greet(me + 2 * plane * ((z + d) % Z - z))
    for src, dst, s in ((wg_hbm, wg, 0), (wu_hbm, wu, 1), (wd_hbm, wd, 2)):
        pltpu.make_async_copy(src.at[0], dst, w_sem.at[s]).start()

    for k, (src, dst) in enumerate(((ql_hbm, ql_ref), (cl_hbm, cl_ref), (cr_hbm, cr_ref))):
        pltpu.make_async_copy(src, dst, in_sem.at[k]).start()

    xs[chip, c, :, pl.ds(0, D)] = normed_ref[...]
    lane = lax.broadcasted_iota(jnp.int32, (R, EXTRA), 1)
    same = lax.broadcasted_iota(jnp.int32, (R, R), 0) == lax.broadcasted_iota(jnp.int32, (R, R), 1)

    def column(ref, k):
        row = jnp.broadcast_to(ref[k : k + 1, :].astype(F32), (R, R))
        return jnp.sum(jnp.where(same, row, 0.0), axis=1, keepdims=True)

    tail = jnp.zeros((R, EXTRA), F32)
    for k in range(top):
        tail = jnp.where(lane == k, column(ids_ref, k), tail)
        tail = jnp.where(lane == top + k, column(lev_ref, k), tail)
    xs[chip, c, :, pl.ds(D, EXTRA)] = tail.astype(BF)

    pl.semaphore_wait(barrier, Z - 1 + (3 if planar else 1))

    pa = ag_rs.shape[1]
    wa = (D + EXTRA) // pa

    def ag(i, p, way, dev):
        part = xs.at[i, c, :, pl.ds(p * wa, wa)]
        return pltpu.make_async_remote_copy(
            part, part, ag_ss.at[way, i, p], ag_rs.at[i, p], device_id={"expert": dev}
        )

    def ag_core(i, cc):
        return pltpu.make_async_remote_copy(
            xs.at[i, cc], xs.at[i, cc], agc_ss.at[i], agc_rs.at[i], device_id={"expert": peer_c}
        )

    def got(i, p):
        ag(i, p, SIDE_A, peer_a).wait_recv()

    def ag_z(zz, p, way, dev):
        i = at(zz, a, b)
        part = xs.at[i, c, :, pl.ds(p * wa, wa)]
        return pltpu.make_async_remote_copy(
            part, part, agz_ss.at[way, zz, p], ag_rs.at[i, p], device_id={"expert": dev}
        )

    def go_up(zz, p):
        pl.when(z < Z - 1)(lambda: ag_z(zz, p, 0, me + 2 * plane).start())

    def go_down(zz, p):
        pl.when(z > 0)(lambda: ag_z(zz, p, 1, me - 2 * plane).start())

    def share(zz, wait, *onward):
        i = at(zz, a, b)
        for p in range(pa):
            if wait:
                got(i, p)
            for step in onward:
                step(zz, p)
            if planar:
                ag(i, p, SIDE_A, peer_a).start()
                ag(i, p, SIDE_B, peer_b).start()
        ag_core(i, c).start()

    def column_dev(zz):
        return me + 2 * plane * (zz - z)

    share(z, False, go_up, go_down)

    qr = qr_ref[...].astype(F32)
    heads, rope = ql_ref.shape[1], cr_ref.shape[1]
    for h in range(heads):
        rq[h * R : (h + 1) * R, :rope] = qr[:, h * rope : (h + 1) * rope]

    lmax = cl_ref.shape[1]
    for k, (src, dst) in enumerate(((ql_hbm, ql_ref), (cl_hbm, cl_ref), (cr_hbm, cr_ref))):
        pltpu.make_async_copy(src, dst, in_sem.at[k]).wait()

    def attend(t):
        keys = cl_ref[t]
        rope_q = rq[pl.ds(t, heads, stride=R), :rope].astype(BF)
        s = lax.dot_general(ql_ref[t], keys, (((1,), (1,)), ((), ())), preferred_element_type=F32)
        s = s + jnp.dot(rope_q, cr_ref[t], preferred_element_type=F32)
        s = s * score_scale
        seen = lax.broadcasted_iota(jnp.int32, (heads, lmax), 1) < len_ref[t]
        s = jnp.where(seen, s, -1e30)
        e = jnp.where(seen, jnp.exp(s - jnp.max(s, axis=-1, keepdims=True)), 0.0)
        p = (e / jnp.sum(e, axis=-1, keepdims=True)).astype(BF)
        att_ref[t] = jnp.dot(p, keys, preferred_element_type=F32).astype(BF)

    def from_a(zz):
        i = at(zz, 1 - a, b)
        for p in range(pa):
            got(i, p)
            ag(i, p, SIDE_B, peer_b).start()
        ag_core(i, c).start()

    if planar:
        from_a(z)

    def z_step(d, carry):
        pl.when(z - d >= 0)(lambda: share(z - d, True, go_up))
        pl.when(z + d < Z)(lambda: share(z + d, True, go_down))
        if planar:
            pl.when(z - d >= 0)(lambda: from_a(z - d))
            pl.when(z + d < Z)(lambda: from_a(z + d))
        return carry

    lax.fori_loop(1, Z, z_step, 0)

    if planar:
        def from_b(k, carry):
            attend(k)
            i = at((z + k // 2) % Z, k % 2, 1 - b)
            for p in range(pa):
                got(i, p)
            ag_core(i, c).start()
            return carry

        lax.fori_loop(0, 2 * Z, from_b, 0)
        first = min(2 * Z, R)
    else:
        first = 0
    for t in range(first, R):
        attend(t)

    pltpu.make_async_copy(att_ref, att_hbm, out_sem).start()

    def from_core(i, carry):
        ag_core(i, 1 - c).wait_recv()
        return carry

    lax.fori_loop(0, chips, from_core, 0)

    for src, dst, s in ((wg_hbm, wg, 0), (wu_hbm, wu, 1), (wd_hbm, wd, 2)):
        pltpu.make_async_copy(src.at[0], dst, w_sem.at[s]).wait()
    rows = n * R
    kc = 3584
    gacc[...] = jnp.zeros_like(gacc)
    uacc[...] = jnp.zeros_like(uacc)

    def k_step(k, carry):
        ks = pl.ds(pl.multiple_of(k * kc, kc), kc)
        xk = xs[:, :, :, ks].astype(F32).reshape(rows, kc).astype(BF)
        gacc[...] += jnp.dot(xk, wg[ks, :], preferred_element_type=F32)
        uacc[...] += jnp.dot(xk, wu[ks, :], preferred_element_type=F32)
        return carry

    lax.fori_loop(0, D // kc, k_step, 0)
    g = gacc[...]
    hidden = (g / (1.0 + jnp.exp(-g)) * uacc[...]).astype(BF)
    h3[...] = hidden.astype(F32).reshape(chips, 2, R, F)

    mine = place_ref[me].astype(F32)
    info = xs[:, :, :, pl.ds(D, EXTRA)].astype(F32).reshape(rows, EXTRA)
    levels = [info[:, top + k : top + k + 1] for k in range(top)]
    total = functools.reduce(lambda p, q: p + q, levels)
    coef = jnp.zeros((rows, 1), F32)
    for k in range(top):
        coef = coef + jnp.where(info[:, k : k + 1] == mine, route_scale * levels[k] / total, 0.0)
    cf[...] = jnp.broadcast_to(coef, (rows, EXTRA)).reshape(chips, 2, R, EXTRA)

    nc = 1792

    def down_half(cc):
        hh = h3[:, cc].reshape(chips * R, F).astype(BF)
        scale = cf[:, cc].reshape(chips * R, EXTRA)[:, :1]

        def n_step(k, carry):
            ns = pl.ds(pl.multiple_of(k * nc, nc), nc)
            p = jnp.dot(hh, wd[:, ns], preferred_element_type=F32).astype(BF).astype(F32)
            acc[:, cc, :, ns] = (p * scale).reshape(chips, R, nc).astype(BF)
            return carry

        lax.fori_loop(0, D // nc, n_step, 0)

    pr = rz_s.shape[1]
    wr = D // pr

    def cols(p):
        return pl.ds(p * wr, wr)

    def to_core(i):
        return pltpu.make_async_remote_copy(
            acc.at[i, 1 - c], rc.at[i], rsc_ss.at[i], rc_s.at[i], device_id={"expert": peer_c}
        )

    def to_b(zz, aa, p):
        i = at(zz, aa, 1 - b)
        return pltpu.make_async_remote_copy(
            acc.at[i, c, :, cols(p)], rb.at[zz, aa, :, cols(p)], rs_ss.at[SIDE_B, i, p],
            rb_s.at[zz, aa, p], device_id={"expert": peer_b},
        )

    def to_a(zz, p):
        i = at(zz, 1 - a, b)
        return pltpu.make_async_remote_copy(
            acc.at[i, c, :, cols(p)], ra.at[zz, :, cols(p)], rs_ss.at[SIDE_A, i, p],
            ra_s.at[zz, p], device_id={"expert": peer_a},
        )

    def to_z(zz, p):
        return pltpu.make_async_remote_copy(
            acc.at[at(zz, a, b), c, :, cols(p)], rz.at[z, :, cols(p)], rsz_ss.at[zz, p],
            rz_s.at[z, p], device_id={"expert": column_dev(zz)},
        )

    def from_z(zz, p):
        return pltpu.make_async_remote_copy(
            acc.at[chip, c, :, cols(p)], rz.at[zz, :, cols(p)], rsz_ss.at[zz, p],
            rz_s.at[zz, p], device_id={"expert": column_dev(zz)},
        )

    down_half(1 - c)

    def far(k):
        return (z + 1 + k) % Z

    def core_send(k, carry):
        if planar:
            q = k % (chips // 2)
            zz, other = far(q // 2), 1 - q % 2
            away = 1 - k // (chips // 2)
            aa = (1 - 2 * a) * away + a
            bb = (1 - 2 * b) * other + b
            to_core(at(zz, aa, bb)).start()
        else:
            to_core(far(k)).start()
        return carry

    lax.fori_loop(0, chips, core_send, 0)
    down_half(c)

    def plus(*terms):
        return functools.reduce(lambda p, q: p + q, [t.astype(F32) for t in terms])

    if planar:
        def b_send(k, carry):
            zz = far(k // 2)
            aa = (1 - 2 * a) * (1 - k % 2) + a
            i = at(zz, aa, 1 - b)
            to_core(i).wait_recv()
            acc[i, c] = plus(acc[i, c], rc[i]).astype(BF)
            for p in range(pr):
                to_b(zz, aa, p).start()
            return carry

        lax.fori_loop(0, 2 * Z, b_send, 0)

        def a_send(k):
            zz = far(k)
            i = at(zz, 1 - a, b)
            to_core(i).wait_recv()
            for p in range(pr):
                to_b(zz, 1 - a, p).wait_recv()
                cp = cols(p)
                acc[i, c, :, cp] = plus(acc[i, c, :, cp], rc[i, :, cp], rb[zz, 1 - a, :, cp]).astype(BF)
                to_a(zz, p).start()

        a_send(0)

    def column_sum(zz, p):
        i = at(zz, a, b)
        cp = cols(p)
        if planar:
            to_b(zz, a, p).wait_recv()
            to_a(zz, p).wait_recv()
            return plus(acc[i, c, :, cp], rc[i, :, cp], rb[zz, a, :, cp], ra[zz, :, cp])
        return plus(acc[i, c, :, cp], rc[i, :, cp])

    def z_send(k, carry):
        if planar:
            a_send(k + 1)
        zz = far(k)
        to_core(at(zz, a, b)).wait_recv()
        for p in range(pr):
            acc[at(zz, a, b), c, :, cols(p)] = column_sum(zz, p).astype(BF)
            to_z(zz, p).start()
        return carry

    lax.fori_loop(0, Z - 1, z_send, 0)
    to_core(chip).wait_recv()
    for p in range(pr):
        result = column_sum(z, p)
        for d in range(1, Z):
            zz = (z + d) % Z
            from_z(zz, p).wait_recv()
            result = result + rz[zz, :, cols(p)].astype(F32)
        moe_ref[:, cols(p)] = result.astype(BF)

    pltpu.make_async_copy(att_ref, att_hbm, out_sem).wait()

    def core_done(i, carry):
        ag_core(i, c).wait_send()
        to_core(i).wait_send()
        return carry

    lax.fori_loop(0, chips, core_done, 0)

    def z_done(zz, carry):
        i = at(zz, a, b)

        @pl.when(zz != z)
        def _():
            for p in range(pr):
                to_z(zz, p).wait_send()

        for p in range(pa):
            pl.when((zz <= z) & (z < Z - 1))(lambda: ag_z(zz, p, 0, me + 2 * plane).wait_send())
            pl.when((zz >= z) & (z > 0))(lambda: ag_z(zz, p, 1, me - 2 * plane).wait_send())
        if planar:
            for p in range(pa):
                ag(i, p, SIDE_A, peer_a).wait_send()
                for aa in range(2):
                    ag(at(zz, aa, b), p, SIDE_B, peer_b).wait_send()
            for p in range(pr):
                to_a(zz, p).wait_send()
                for aa in range(2):
                    to_b(zz, aa, p).wait_send()
        return carry

    lax.fori_loop(0, Z, z_done, 0)


def on_line(
    normed, expert_ids, gate_levels, placement, w_gate, w_up, w_down,
    q_latent, q_rope, cache_latent, cache_rope, lengths,
):
    n = lax.axis_size("expert")
    Z, Y, X = chip_grid(n)
    chips = n // 2
    R, D = normed.shape
    F = w_gate.shape[2]
    heads = q_latent.shape[1]
    vmem = pl.BlockSpec(memory_space=pltpu.VMEM)
    smem = pl.BlockSpec(memory_space=pltpu.SMEM)
    hbm = pl.BlockSpec(memory_space=pl.ANY)
    dma = pltpu.SemaphoreType.DMA
    side = Z if Y * X > 1 else 1
    pa, pr = parts(D + EXTRA, PA), parts(D, PR)
    return pl.pallas_call(
        functools.partial(line_body, n),
        out_shape=(
            jax.ShapeDtypeStruct((R, D), BF),
            jax.ShapeDtypeStruct(q_latent.shape, BF),
        ),
        in_specs=[vmem, vmem, vmem, smem, smem, hbm, hbm, hbm, hbm, vmem, hbm, hbm],
        out_specs=(vmem, hbm),
        scratch_shapes=[
            pltpu.VMEM((chips, 2, R, D + EXTRA), BF),
            pltpu.VMEM((chips, 2, R, D), BF),
            pltpu.VMEM((chips, R, D), BF),
            pltpu.VMEM((side, 2, R, D), BF),
            pltpu.VMEM((side, R, D), BF),
            pltpu.VMEM((Z, R, D), BF),
            pltpu.VMEM((D, F), BF),
            pltpu.VMEM((D, F), BF),
            pltpu.VMEM((F, D), BF),
            pltpu.VMEM((chips, 2, R, F), F32),
            pltpu.VMEM((chips, 2, R, EXTRA), F32),
            pltpu.VMEM((heads * R, 128), F32),
            pltpu.VMEM((n * R, F), F32),
            pltpu.VMEM((n * R, F), F32),
            pltpu.VMEM(q_latent.shape, BF),
            pltpu.VMEM(cache_latent.shape, BF),
            pltpu.VMEM(cache_rope.shape, BF),
            pltpu.VMEM(q_latent.shape, BF),
            dma((3,)),
            dma((3,)),
            dma,
            dma((2, chips, pa)),
            dma((chips, pa)),
            dma((2, Z, pa)),
            dma((chips,)),
            dma((chips,)),
            dma((2, chips, pr)),
            dma((Z, pr)),
            dma((chips,)),
            dma((chips,)),
            dma((side, 2, pr)),
            dma((side, pr)),
            dma((Z, pr)),
        ],
        compiler_params=pltpu.CompilerParams(
            collective_id=0, has_side_effects=True, vmem_limit_bytes=60 << 20
        ),
        cost_estimate=pl.CostEstimate(flops=3 * 10**9, bytes_accessed=13 * 10**6, transcendentals=300000),
    )(
        normed, expert_ids.T, gate_levels.T, lengths, placement, w_gate, w_up, w_down,
        q_latent, q_rope, cache_latent, cache_rope,
    )


AG_PARTS = 3
RS_PARTS = 2


def grid_body(
    n,
    normed_hbm, ids_hbm, lev_hbm, len_hbm, place_hbm, wg_hbm, wu_hbm, wd_hbm,
    ql_hbm, qr_hbm, cl_hbm, cr_hbm,
    moe_ref, att_ref,
    xs, acc, rc, rb, ra, rz, rx, wg, wu, wd, own, ids, lev, qr, rq, ql, cl, cr, lens, place,
    in_sem, w_sem,
    ag_ss, ag_rs, agc_rs, rs_ss, rc_s, rb_s, ra_s, rz_s, rx_s,
):
    Z, Y, X = chip_grid(n)
    plane = Y * X
    R, D = own.shape
    W = D + EXTRA
    F = wg.shape[1]
    top = ids.shape[0]
    me = lax.axis_index("expert")
    c = me % 2
    chip = me // 2
    z = chip // plane
    y = (chip % plane) // X
    x = chip % X
    a = x * (1 - c) + y * c
    b = y * (1 - c) + x * c
    sa = (1 - c) + X * c
    sb = X * (1 - c) + c
    near = z + 1 - 2 * (z % 2)
    far = (z + 2) % Z
    far2 = far + 1 - 2 * (far % 2)
    peer_a = me + 2 * (1 - 2 * a) * sa
    peer_b = me + 2 * (1 - 2 * b) * sb
    peer_c = 2 * chip + 1 - c
    peer_n = me + 2 * plane * (near - z)
    peer_f = me + 2 * plane * (far - z)

    def spot(zz, bb, aa):
        return zz // 2, 4 * (zz % 2) + 2 * bb + aa

    barrier = pltpu.get_barrier_semaphore()
    for dev in (peer_c, peer_a, peer_b, peer_n, peer_f):
        pl.semaphore_signal(barrier, inc=1, device_id={"expert": dev})

    loads = [
        pltpu.make_async_copy(src, dst, in_sem.at[k])
        for k, (src, dst) in enumerate((
            (normed_hbm, own), (ids_hbm, ids), (lev_hbm, lev), (len_hbm, lens), (place_hbm, place),
            (qr_hbm, qr), (ql_hbm, ql), (cl_hbm, cl), (cr_hbm, cr),
        ))
    ]
    for load in loads:
        load.start()
    weights = [
        pltpu.make_async_copy(src.at[0], dst, w_sem.at[k])
        for k, (src, dst) in enumerate(((wg_hbm, wg), (wu_hbm, wu), (wd_hbm, wd)))
    ]
    for load in weights:
        load.start()
    for load in loads[:3]:
        load.wait()

    xs[(c, *spot(z, b, a), slice(None), pl.ds(0, D))] = own[...]
    lane = lax.broadcasted_iota(jnp.int32, (R, EXTRA), 1)
    same = lax.broadcasted_iota(jnp.int32, (R, R), 0) == lax.broadcasted_iota(jnp.int32, (R, R), 1)

    def column(ref, k):
        row = jnp.broadcast_to(ref[k : k + 1, :].astype(F32), (R, R))
        return jnp.sum(jnp.where(same, row, 0.0), axis=1, keepdims=True)

    tail = jnp.zeros((R, EXTRA), F32)
    for k in range(top):
        tail = jnp.where(lane == k, column(ids, k), tail)
        tail = jnp.where(lane == top + k, column(lev, k), tail)
    xs[(c, *spot(z, b, a), slice(None), pl.ds(D, EXTRA))] = tail.astype(BF)

    pl.semaphore_wait(barrier, 5)

    pa = ag_rs.shape[-1]
    wa = W // pa
    TO_A, TO_B, TO_C, TO_N, TO_F = range(5)
    peers = (peer_a, peer_b, peer_c, peer_n, peer_f)

    def ag(zz, bb, aa, p, way):
        g, j = spot(zz, bb, aa)
        part = xs.at[c, g, j, :, pl.ds(p * wa, wa)]
        return pltpu.make_async_remote_copy(
            part, part, ag_ss.at[way], ag_rs.at[g, j, p], device_id={"expert": peers[way]}
        )

    def got(zz, bb, aa, p):
        ag(zz, bb, aa, p, TO_A).wait_recv()

    def core_one(zz, bb, aa, cc):
        g, j = spot(zz, bb, aa)
        part = xs.at[cc, g, j]
        return pltpu.make_async_remote_copy(
            part, part, ag_ss.at[TO_C], agc_rs.at[g, j], device_id={"expert": peer_c}
        )

    def pass_on(zz, bb, aa, ways, wait=True, core=True):
        for p in range(pa):
            if wait:
                got(zz, bb, aa, p)
            for way in ways:
                ag(zz, bb, aa, p, way).start()
        if core:
            core_one(zz, bb, aa, c).start()

    pass_on(z, b, a, (TO_A, TO_B, TO_N, TO_F), wait=False)

    for load in loads[3:]:
        load.wait()
    heads, rope = ql.shape[1], cr.shape[1]
    lmax = cl.shape[1]
    queries = qr[...].astype(F32)
    for h in range(heads):
        rq[h * R : (h + 1) * R, :rope] = queries[:, h * rope : (h + 1) * rope]

    def attend(t):
        keys = cl[t]
        rope_q = rq[pl.ds(t, heads, stride=R), :rope].astype(BF)
        s = lax.dot_general(ql[t], keys, (((1,), (1,)), ((), ())), preferred_element_type=F32)
        s = s + jnp.dot(rope_q, cr[t], preferred_element_type=F32)
        s = s * score_scale
        seen = lax.broadcasted_iota(jnp.int32, (heads, lmax), 1) < lens[t]
        s = jnp.where(seen, s, -1e30)
        e = jnp.where(seen, jnp.exp(s - jnp.max(s, axis=-1, keepdims=True)), 0.0)
        p = (e / jnp.sum(e, axis=-1, keepdims=True)).astype(BF)
        att_ref[t] = jnp.dot(p, keys, preferred_element_type=F32).astype(BF)

    attend(0)
    attend(1)
    pass_on(near, b, a, (TO_A, TO_B))
    pass_on(z, b, 1 - a, (TO_B,))
    attend(2)
    attend(3)
    pass_on(far, b, a, (TO_N,), core=False)
    pass_on(near, b, 1 - a, (TO_B,))
    pass_on(far, b, a, (TO_A, TO_B), wait=False)
    attend(4)
    attend(5)
    pass_on(far2, b, a, (TO_A, TO_B))
    attend(6)
    attend(7)
    for zz in (z, near):
        for aa in range(2):
            pass_on(zz, 1 - b, aa, ())

    pair = z // 2
    pr = rc_s.shape[-1]
    wr = D // pr
    rows = 8 * 2 * R

    def cols(k):
        return pl.ds(k * wr, wr)

    def group(q):
        return (pair + q) % 2

    def planes(q):
        return ((near, z), (far2, far))[q]

    def low(q, d):
        return planes(q)[d] % 2

    def to_core(q, d, k):
        part = pl.ds(4 * low(q, d), 4)
        return pltpu.make_async_remote_copy(
            acc.at[1 - c, group(q), part, :, cols(k)], rc.at[group(q), part, :, cols(k)],
            rs_ss.at[TO_C, q, d, k], rc_s.at[q, d, k], device_id={"expert": peer_c},
        )

    def to_b(q, d, k):
        return pltpu.make_async_remote_copy(
            acc.at[c, group(q), pl.ds(4 * low(q, d) + 2 * (1 - b), 2), :, cols(k)],
            rb.at[group(q), pl.ds(2 * low(q, d), 2), :, cols(k)],
            rs_ss.at[TO_B, q, d, k], rb_s.at[q, d, k], device_id={"expert": peer_b},
        )

    def to_a(q, d, k):
        zz = planes(q)[d]
        return pltpu.make_async_remote_copy(
            acc.at[(c, *spot(zz, b, 1 - a), slice(None), cols(k))], ra.at[group(q), low(q, d), :, cols(k)],
            rs_ss.at[TO_A, q, d, k], ra_s.at[q, d, k], device_id={"expert": peer_a},
        )

    def to_near(q, k):
        zz, dst, sem = ((near, rz.at[0, :, cols(k)], rz_s.at[0, k]), (far2, rx.at[:, cols(k)], rx_s.at[k]))[q]
        return pltpu.make_async_remote_copy(
            acc.at[(c, *spot(zz, b, a), slice(None), cols(k))], dst, rs_ss.at[TO_N, q, 0, k], sem, device_id={"expert": peer_n},
        )

    def to_far(k):
        return pltpu.make_async_remote_copy(
            acc.at[(c, *spot(far, b, a), slice(None), cols(k))], rz.at[1, :, cols(k)], rs_ss.at[TO_F, 0, 0, k], rz_s.at[1, k],
            device_id={"expert": peer_f},
        )

    def gathered(q):
        for d in range(2):
            for bb in range(2):
                for aa in range(2):
                    core_one(2 * ((pair + q) % 2) + d, bb, aa, 1 - c).wait_recv()

    kc = D // 2

    def compute(q):
        gq = group(q)
        g = jnp.zeros((rows, F), F32)
        u = jnp.zeros((rows, F), F32)
        for k in range(D // kc):
            ks = pl.ds(k * kc, kc)
            xk = xs[:, gq, :, :, ks].astype(F32).reshape(rows, kc).astype(BF)
            g += jnp.dot(xk, wg[ks, :], preferred_element_type=F32)
            u += jnp.dot(xk, wu[ks, :], preferred_element_type=F32)
        hidden = (g / (1.0 + jnp.exp(-g)) * u).astype(BF)
        mine = place[me].astype(F32)
        info = xs[:, gq, :, :, pl.ds(D, EXTRA)].astype(F32).reshape(rows, EXTRA)
        levels = [info[:, top + k : top + k + 1] for k in range(top)]
        total = functools.reduce(lambda p, q: p + q, levels)
        coef = jnp.zeros((rows, 1), F32)
        for k in range(top):
            coef = coef + jnp.where(info[:, k : k + 1] == mine, route_scale * levels[k] / total, 0.0)
        for k in range(pr):
            p = jnp.dot(hidden, wd[:, cols(k)], preferred_element_type=F32).astype(BF).astype(F32)
            acc[:, gq, :, :, cols(k)] = (p * coef).reshape(2, 8, R, wr).astype(BF)
            for d in range(2):
                to_core(q, d, k).start()

    def plus(*terms):
        return functools.reduce(lambda p, q: p + q, [t.astype(F32) for t in terms])

    def send_b(q, d, k):
        to_core(q, d, k).wait_recv()
        cp, gq = cols(k), group(q)
        part = pl.ds(4 * low(q, d) + 2 * (1 - b), 2)
        acc[c, gq, part, :, cp] = plus(acc[c, gq, part, :, cp], rc[gq, part, :, cp]).astype(BF)
        to_b(q, d, k).start()

    def send_a(q, d, k):
        to_b(q, d, k).wait_recv()
        cp = cols(k)
        g, j = spot(planes(q)[d], b, 1 - a)
        acc[c, g, j, :, cp] = plus(
            acc[c, g, j, :, cp], rc[g, j, :, cp], rb[g, 2 * low(q, d) + 1 - a, :, cp]
        ).astype(BF)
        to_a(q, d, k).start()

    def column_sum(zz, k):
        cp = cols(k)
        g, j = spot(zz, b, a)
        return plus(acc[c, g, j, :, cp], rc[g, j, :, cp], rb[g, 2 * (zz % 2) + a, :, cp], ra[g, zz % 2, :, cp])

    def send_near(q, k):
        to_a(q, 0, k).wait_recv()
        zz = planes(q)[0]
        acc[(c, *spot(zz, b, a), slice(None), cols(k))] = column_sum(zz, k).astype(BF)
        to_near(q, k).start()

    def send_far(k):
        to_a(1, 1, k).wait_recv()
        to_near(1, k).wait_recv()
        acc[(c, *spot(far, b, a), slice(None), cols(k))] = plus(column_sum(far, k), rx[:, cols(k)]).astype(BF)
        to_far(k).start()

    def finish(k):
        to_a(0, 1, k).wait_recv()
        to_near(0, k).wait_recv()
        to_far(k).wait_recv()
        moe_ref[:, cols(k)] = plus(column_sum(z, k), rz[0, :, cols(k)], rz[1, :, cols(k)]).astype(BF)

    for load in weights:
        load.wait()
    chunks = [(d, k) for d in range(2) for k in range(pr)]
    gathered(0)
    compute(0)
    for zz in (far, far2):
        pass_on(zz, b, 1 - a, (TO_B,))
    for d, k in chunks:
        send_b(0, d, k)
    for zz in (far, far2):
        for aa in range(2):
            pass_on(zz, 1 - b, aa, ())
    gathered(1)
    compute(1)
    for d, k in chunks:
        send_a(0, d, k)
    for d, k in chunks:
        send_b(1, d, k)
    for k in range(pr):
        send_near(0, k)
    for k in range(pr):
        send_a(1, 0, k)
    for k in range(pr):
        send_near(1, k)
    for k in range(pr):
        send_a(1, 1, k)
    for k in range(pr):
        send_far(k)
    for k in range(pr):
        finish(k)

    for part, way in (
        (xs.at[c], TO_C), (xs.at[c, :, pl.ds(0, 4)], TO_B), (xs.at[c, :, pl.ds(0, 2)], TO_A),
        (xs.at[c, 0, pl.ds(0, 2)], TO_N), (xs.at[c, 0, 0], TO_F),
    ):
        pltpu.make_async_copy(part, part, ag_ss.at[way]).wait()
    for k in range(pr):
        for q in range(2):
            for d in range(2):
                to_core(q, d, k).wait_send()
                to_b(q, d, k).wait_send()
                to_a(q, d, k).wait_send()
            to_near(q, k).wait_send()
        to_far(k).wait_send()


def on_grid(
    normed, expert_ids, gate_levels, placement, w_gate, w_up, w_down,
    q_latent, q_rope, cache_latent, cache_rope, lengths,
):
    n = lax.axis_size("expert")
    Z, Y, X = chip_grid(n)
    R, D = normed.shape
    F = w_gate.shape[2]
    heads, top = q_latent.shape[1], expert_ids.shape[1]
    vmem = pl.BlockSpec(memory_space=pltpu.VMEM)
    hbm = pl.BlockSpec(memory_space=pl.ANY)
    dma = pltpu.SemaphoreType.DMA
    pa, pr = AG_PARTS, RS_PARTS
    return pl.pallas_call(
        functools.partial(grid_body, n),
        out_shape=(pltpu.VMEM((R, D), BF), pltpu.VMEM(q_latent.shape, BF)),
        in_specs=[hbm] * 12,
        out_specs=(vmem, vmem),
        scratch_shapes=[
            pltpu.VMEM((2, Z // 2, 8, R, D + EXTRA), BF),
            pltpu.VMEM((2, Z // 2, 8, R, D), BF),
            pltpu.VMEM((Z // 2, 8, R, D), BF),
            pltpu.VMEM((Z // 2, 4, R, D), BF),
            pltpu.VMEM((Z // 2, 2, R, D), BF),
            pltpu.VMEM((2, R, D), BF),
            pltpu.VMEM((R, D), BF),
            pltpu.VMEM((D, F), BF),
            pltpu.VMEM((D, F), BF),
            pltpu.VMEM((F, D), BF),
            pltpu.VMEM((R, D), BF),
            pltpu.VMEM((top, R), jnp.int32),
            pltpu.VMEM((top, R), jnp.int32),
            pltpu.VMEM(q_rope.shape, BF),
            pltpu.VMEM((heads * R, 128), F32),
            pltpu.VMEM(q_latent.shape, BF),
            pltpu.VMEM(cache_latent.shape, BF),
            pltpu.VMEM(cache_rope.shape, BF),
            pltpu.SMEM((R,), jnp.int32),
            pltpu.SMEM((n,), jnp.int32),
            dma((9,)),
            dma((3,)),
            dma((5,)),
            dma((Z // 2, 8, pa)),
            dma((Z // 2, 8)),
            dma((5, 2, 2, pr)),
            dma((2, 2, pr)),
            dma((2, 2, pr)),
            dma((2, 2, pr)),
            dma((2, pr)),
            dma((pr,)),
        ],
        compiler_params=pltpu.CompilerParams(
            collective_id=0, has_side_effects=True, vmem_limit_bytes=60 << 20
        ),
        cost_estimate=pl.CostEstimate(flops=3 * 10**9, bytes_accessed=13 * 10**6, transcendentals=300000),
    )(
        normed, expert_ids.T, gate_levels.T, lengths, placement, w_gate, w_up, w_down,
        q_latent, q_rope, cache_latent, cache_rope,
    )


def per_device(*args):
    n = lax.axis_size("expert")
    Z, Y, X = chip_grid(n)
    return on_grid(*args) if Y * X > 1 else on_line(*args)


def solution(mesh):
    rows = ("groups", "expert")
    in_specs = (
        P(rows, None), P(rows, None), P(rows, None), P(),
        P("expert", None, None), P("expert", None, None), P("expert", None, None),
        P(rows, None, None), P(rows, None), P(rows, None, None), P(rows, None, None), P(rows),
    )
    out_specs = (P(rows, None), P(rows, None, None))
    return jax.shard_map(
        per_device, mesh=mesh, in_specs=in_specs, out_specs=out_specs, check_vma=False
    )
```

```python
import functools

import jax
import jax.numpy as jnp
from jax import lax
from jax.experimental import pallas as pl
from jax.experimental.pallas import tpu as pltpu
from jax.sharding import PartitionSpec as P

score_scale = 192.0 ** (-0.5)
route_scale = 2.5
BF, F32 = jnp.bfloat16, jnp.float32
EXTRA = 128
PA, PR = 3, 2
SIDE_A, SIDE_B = range(2)


def chip_grid(n):
    return (4, 2, 2) if n == 32 else (n // 2, 1, 1)


def parts(cols, most):
    return max(p for p in range(1, most + 1) if cols % (128 * p) == 0)


def line_body(
    n,
    normed_ref, ids_ref, lev_ref, len_ref, place_ref, wg_hbm, wu_hbm, wd_hbm,
    ql_hbm, qr_ref, cl_hbm, cr_hbm,
    moe_ref, att_hbm,
    xs, acc, rc, rb, ra, rz, wg, wu, wd, h3, cf, rq, gacc, uacc, ql_ref, cl_ref, cr_ref, att_ref,
    w_sem, in_sem, out_sem, ag_ss, ag_rs, agz_ss, agc_ss, agc_rs, rs_ss, rsz_ss, rsc_ss, rc_s, rb_s, ra_s, rz_s,
):
    Z, Y, X = chip_grid(n)
    plane = Y * X
    planar = plane > 1
    chips = n // 2
    R, D = normed_ref.shape
    F = wg.shape[1]
    top = ids_ref.shape[0]
    me = lax.axis_index("expert")
    c = me % 2
    chip = me // 2
    z = chip // plane
    y = (chip % plane) // X
    x = chip % X
    a = x * (1 - c) + y * c
    b = y * (1 - c) + x * c
    sa = (1 - c) + X * c
    sb = X * (1 - c) + c
    peer_a = me + 2 * (1 - 2 * a) * sa
    peer_b = me + 2 * (1 - 2 * b) * sb
    peer_c = 2 * chip + 1 - c

    def at(zz, aa, bb):
        if planar:
            return zz * plane + aa * sa + bb * sb
        return zz

    barrier = pltpu.get_barrier_semaphore()

    def greet(dev):
        pl.semaphore_signal(barrier, inc=1, device_id={"expert": dev})

    greet(peer_c)
    if planar:
        greet(peer_a)
        greet(peer_b)
    for d in range(1, Z):
        greet(me + 2 * plane * ((z + d) % Z - z))
    for src, dst, s in ((wg_hbm, wg, 0), (wu_hbm, wu, 1), (wd_hbm, wd, 2)):
        pltpu.make_async_copy(src.at[0], dst, w_sem.at[s]).start()

    for k, (src, dst) in enumerate(((ql_hbm, ql_ref), (cl_hbm, cl_ref), (cr_hbm, cr_ref))):
        pltpu.make_async_copy(src, dst, in_sem.at[k]).start()

    xs[chip, c, :, pl.ds(0, D)] = normed_ref[...]
    lane = lax.broadcasted_iota(jnp.int32, (R, EXTRA), 1)
    same = lax.broadcasted_iota(jnp.int32, (R, R), 0) == lax.broadcasted_iota(jnp.int32, (R, R), 1)

    def column(ref, k):
        row = jnp.broadcast_to(ref[k : k + 1, :].astype(F32), (R, R))
        return jnp.sum(jnp.where(same, row, 0.0), axis=1, keepdims=True)

    tail = jnp.zeros((R, EXTRA), F32)
    for k in range(top):
        tail = jnp.where(lane == k, column(ids_ref, k), tail)
        tail = jnp.where(lane == top + k, column(lev_ref, k), tail)
    xs[chip, c, :, pl.ds(D, EXTRA)] = tail.astype(BF)

    pl.semaphore_wait(barrier, Z - 1 + (3 if planar else 1))

    pa = ag_rs.shape[1]
    wa = (D + EXTRA) // pa

    def ag(i, p, way, dev):
        part = xs.at[i, c, :, pl.ds(p * wa, wa)]
        return pltpu.make_async_remote_copy(
            part, part, ag_ss.at[way, i, p], ag_rs.at[i, p], device_id={"expert": dev}
        )

    def ag_core(i, cc):
        return pltpu.make_async_remote_copy(
            xs.at[i, cc], xs.at[i, cc], agc_ss.at[i], agc_rs.at[i], device_id={"expert": peer_c}
        )

    def got(i, p):
        ag(i, p, SIDE_A, peer_a).wait_recv()

    def ag_z(zz, p, way, dev):
        i = at(zz, a, b)
        part = xs.at[i, c, :, pl.ds(p * wa, wa)]
        return pltpu.make_async_remote_copy(
            part, part, agz_ss.at[way, zz, p], ag_rs.at[i, p], device_id={"expert": dev}
        )

    def go_up(zz, p):
        pl.when(z < Z - 1)(lambda: ag_z(zz, p, 0, me + 2 * plane).start())

    def go_down(zz, p):
        pl.when(z > 0)(lambda: ag_z(zz, p, 1, me - 2 * plane).start())

    def share(zz, wait, *onward):
        i = at(zz, a, b)
        for p in range(pa):
            if wait:
                got(i, p)
            for step in onward:
                step(zz, p)
            if planar:
                ag(i, p, SIDE_A, peer_a).start()
                ag(i, p, SIDE_B, peer_b).start()
        ag_core(i, c).start()

    def column_dev(zz):
        return me + 2 * plane * (zz - z)

    share(z, False, go_up, go_down)

    qr = qr_ref[...].astype(F32)
    heads, rope = ql_ref.shape[1], cr_ref.shape[1]
    for h in range(heads):
        rq[h * R : (h + 1) * R, :rope] = qr[:, h * rope : (h + 1) * rope]

    lmax = cl_ref.shape[1]
    for k, (src, dst) in enumerate(((ql_hbm, ql_ref), (cl_hbm, cl_ref), (cr_hbm, cr_ref))):
        pltpu.make_async_copy(src, dst, in_sem.at[k]).wait()

    def attend(t):
        keys = cl_ref[t]
        rope_q = rq[pl.ds(t, heads, stride=R), :rope].astype(BF)
        s = lax.dot_general(ql_ref[t], keys, (((1,), (1,)), ((), ())), preferred_element_type=F32)
        s = s + jnp.dot(rope_q, cr_ref[t], preferred_element_type=F32)
        s = s * score_scale
        seen = lax.broadcasted_iota(jnp.int32, (heads, lmax), 1) < len_ref[t]
        s = jnp.where(seen, s, -1e30)
        e = jnp.where(seen, jnp.exp(s - jnp.max(s, axis=-1, keepdims=True)), 0.0)
        p = (e / jnp.sum(e, axis=-1, keepdims=True)).astype(BF)
        att_ref[t] = jnp.dot(p, keys, preferred_element_type=F32).astype(BF)

    def from_a(zz):
        i = at(zz, 1 - a, b)
        for p in range(pa):
            got(i, p)
            ag(i, p, SIDE_B, peer_b).start()
        ag_core(i, c).start()

    if planar:
        from_a(z)

    def z_step(d, carry):
        pl.when(z - d >= 0)(lambda: share(z - d, True, go_up))
        pl.when(z + d < Z)(lambda: share(z + d, True, go_down))
        if planar:
            pl.when(z - d >= 0)(lambda: from_a(z - d))
            pl.when(z + d < Z)(lambda: from_a(z + d))
        return carry

    lax.fori_loop(1, Z, z_step, 0)

    if planar:
        def from_b(k, carry):
            attend(k)
            i = at((z + k // 2) % Z, k % 2, 1 - b)
            for p in range(pa):
                got(i, p)
            ag_core(i, c).start()
            return carry

        lax.fori_loop(0, 2 * Z, from_b, 0)
        first = min(2 * Z, R)
    else:
        first = 0
    for t in range(first, R):
        attend(t)

    pltpu.make_async_copy(att_ref, att_hbm, out_sem).start()

    def from_core(i, carry):
        ag_core(i, 1 - c).wait_recv()
        return carry

    lax.fori_loop(0, chips, from_core, 0)

    for src, dst, s in ((wg_hbm, wg, 0), (wu_hbm, wu, 1), (wd_hbm, wd, 2)):
        pltpu.make_async_copy(src.at[0], dst, w_sem.at[s]).wait()
    rows = n * R
    kc = 3584
    gacc[...] = jnp.zeros_like(gacc)
    uacc[...] = jnp.zeros_like(uacc)

    def k_step(k, carry):
        ks = pl.ds(pl.multiple_of(k * kc, kc), kc)
        xk = xs[:, :, :, ks].astype(F32).reshape(rows, kc).astype(BF)
        gacc[...] += jnp.dot(xk, wg[ks, :], preferred_element_type=F32)
        uacc[...] += jnp.dot(xk, wu[ks, :], preferred_element_type=F32)
        return carry

    lax.fori_loop(0, D // kc, k_step, 0)
    g = gacc[...]
    hidden = (g / (1.0 + jnp.exp(-g)) * uacc[...]).astype(BF)
    h3[...] = hidden.astype(F32).reshape(chips, 2, R, F)

    mine = place_ref[me].astype(F32)
    info = xs[:, :, :, pl.ds(D, EXTRA)].astype(F32).reshape(rows, EXTRA)
    levels = [info[:, top + k : top + k + 1] for k in range(top)]
    total = functools.reduce(lambda p, q: p + q, levels)
    coef = jnp.zeros((rows, 1), F32)
    for k in range(top):
        coef = coef + jnp.where(info[:, k : k + 1] == mine, route_scale * levels[k] / total, 0.0)
    cf[...] = jnp.broadcast_to(coef, (rows, EXTRA)).reshape(chips, 2, R, EXTRA)

    nc = 1792

    def down_half(cc):
        hh = h3[:, cc].reshape(chips * R, F).astype(BF)
        scale = cf[:, cc].reshape(chips * R, EXTRA)[:, :1]

        def n_step(k, carry):
            ns = pl.ds(pl.multiple_of(k * nc, nc), nc)
            p = jnp.dot(hh, wd[:, ns], preferred_element_type=F32).astype(BF).astype(F32)
            acc[:, cc, :, ns] = (p * scale).reshape(chips, R, nc).astype(BF)
            return carry

        lax.fori_loop(0, D // nc, n_step, 0)

    pr = rz_s.shape[1]
    wr = D // pr

    def cols(p):
        return pl.ds(p * wr, wr)

    def to_core(i):
        return pltpu.make_async_remote_copy(
            acc.at[i, 1 - c], rc.at[i], rsc_ss.at[i], rc_s.at[i], device_id={"expert": peer_c}
        )

    def to_b(zz, aa, p):
        i = at(zz, aa, 1 - b)
        return pltpu.make_async_remote_copy(
            acc.at[i, c, :, cols(p)], rb.at[zz, aa, :, cols(p)], rs_ss.at[SIDE_B, i, p],
            rb_s.at[zz, aa, p], device_id={"expert": peer_b},
        )

    def to_a(zz, p):
        i = at(zz, 1 - a, b)
        return pltpu.make_async_remote_copy(
            acc.at[i, c, :, cols(p)], ra.at[zz, :, cols(p)], rs_ss.at[SIDE_A, i, p],
            ra_s.at[zz, p], device_id={"expert": peer_a},
        )

    def to_z(zz, p):
        return pltpu.make_async_remote_copy(
            acc.at[at(zz, a, b), c, :, cols(p)], rz.at[z, :, cols(p)], rsz_ss.at[zz, p],
            rz_s.at[z, p], device_id={"expert": column_dev(zz)},
        )

    def from_z(zz, p):
        return pltpu.make_async_remote_copy(
            acc.at[chip, c, :, cols(p)], rz.at[zz, :, cols(p)], rsz_ss.at[zz, p],
            rz_s.at[zz, p], device_id={"expert": column_dev(zz)},
        )

    down_half(1 - c)

    def far(k):
        return (z + 1 + k) % Z

    def core_send(k, carry):
        if planar:
            q = k % (chips // 2)
            zz, other = far(q // 2), 1 - q % 2
            away = 1 - k // (chips // 2)
            aa = (1 - 2 * a) * away + a
            bb = (1 - 2 * b) * other + b
            to_core(at(zz, aa, bb)).start()
        else:
            to_core(far(k)).start()
        return carry

    lax.fori_loop(0, chips, core_send, 0)
    down_half(c)

    def plus(*terms):
        return functools.reduce(lambda p, q: p + q, [t.astype(F32) for t in terms])

    if planar:
        def b_send(k, carry):
            zz = far(k // 2)
            aa = (1 - 2 * a) * (1 - k % 2) + a
            i = at(zz, aa, 1 - b)
            to_core(i).wait_recv()
            acc[i, c] = plus(acc[i, c], rc[i]).astype(BF)
            for p in range(pr):
                to_b(zz, aa, p).start()
            return carry

        lax.fori_loop(0, 2 * Z, b_send, 0)

        def a_send(k):
            zz = far(k)
            i = at(zz, 1 - a, b)
            to_core(i).wait_recv()
            for p in range(pr):
                to_b(zz, 1 - a, p).wait_recv()
                cp = cols(p)
                acc[i, c, :, cp] = plus(acc[i, c, :, cp], rc[i, :, cp], rb[zz, 1 - a, :, cp]).astype(BF)
                to_a(zz, p).start()

        a_send(0)

    def column_sum(zz, p):
        i = at(zz, a, b)
        cp = cols(p)
        if planar:
            to_b(zz, a, p).wait_recv()
            to_a(zz, p).wait_recv()
            return plus(acc[i, c, :, cp], rc[i, :, cp], rb[zz, a, :, cp], ra[zz, :, cp])
        return plus(acc[i, c, :, cp], rc[i, :, cp])

    def z_send(k, carry):
        if planar:
            a_send(k + 1)
        zz = far(k)
        to_core(at(zz, a, b)).wait_recv()
        for p in range(pr):
            acc[at(zz, a, b), c, :, cols(p)] = column_sum(zz, p).astype(BF)
            to_z(zz, p).start()
        return carry

    lax.fori_loop(0, Z - 1, z_send, 0)
    to_core(chip).wait_recv()
    for p in range(pr):
        result = column_sum(z, p)
        for d in range(1, Z):
            zz = (z + d) % Z
            from_z(zz, p).wait_recv()
            result = result + rz[zz, :, cols(p)].astype(F32)
        moe_ref[:, cols(p)] = result.astype(BF)

    pltpu.make_async_copy(att_ref, att_hbm, out_sem).wait()

    def core_done(i, carry):
        ag_core(i, c).wait_send()
        to_core(i).wait_send()
        return carry

    lax.fori_loop(0, chips, core_done, 0)

    def z_done(zz, carry):
        i = at(zz, a, b)

        @pl.when(zz != z)
        def _():
            for p in range(pr):
                to_z(zz, p).wait_send()

        for p in range(pa):
            pl.when((zz <= z) & (z < Z - 1))(lambda: ag_z(zz, p, 0, me + 2 * plane).wait_send())
            pl.when((zz >= z) & (z > 0))(lambda: ag_z(zz, p, 1, me - 2 * plane).wait_send())
        if planar:
            for p in range(pa):
                ag(i, p, SIDE_A, peer_a).wait_send()
                for aa in range(2):
                    ag(at(zz, aa, b), p, SIDE_B, peer_b).wait_send()
            for p in range(pr):
                to_a(zz, p).wait_send()
                for aa in range(2):
                    to_b(zz, aa, p).wait_send()
        return carry

    lax.fori_loop(0, Z, z_done, 0)


def on_line(
    normed, expert_ids, gate_levels, placement, w_gate, w_up, w_down,
    q_latent, q_rope, cache_latent, cache_rope, lengths,
):
    n = lax.axis_size("expert")
    Z, Y, X = chip_grid(n)
    chips = n // 2
    R, D = normed.shape
    F = w_gate.shape[2]
    heads = q_latent.shape[1]
    vmem = pl.BlockSpec(memory_space=pltpu.VMEM)
    smem = pl.BlockSpec(memory_space=pltpu.SMEM)
    hbm = pl.BlockSpec(memory_space=pl.ANY)
    dma = pltpu.SemaphoreType.DMA
    side = Z if Y * X > 1 else 1
    pa, pr = parts(D + EXTRA, PA), parts(D, PR)
    return pl.pallas_call(
        functools.partial(line_body, n),
        out_shape=(
            jax.ShapeDtypeStruct((R, D), BF),
            jax.ShapeDtypeStruct(q_latent.shape, BF),
        ),
        in_specs=[vmem, vmem, vmem, smem, smem, hbm, hbm, hbm, hbm, vmem, hbm, hbm],
        out_specs=(vmem, hbm),
        scratch_shapes=[
            pltpu.VMEM((chips, 2, R, D + EXTRA), BF),
            pltpu.VMEM((chips, 2, R, D), BF),
            pltpu.VMEM((chips, R, D), BF),
            pltpu.VMEM((side, 2, R, D), BF),
            pltpu.VMEM((side, R, D), BF),
            pltpu.VMEM((Z, R, D), BF),
            pltpu.VMEM((D, F), BF),
            pltpu.VMEM((D, F), BF),
            pltpu.VMEM((F, D), BF),
            pltpu.VMEM((chips, 2, R, F), F32),
            pltpu.VMEM((chips, 2, R, EXTRA), F32),
            pltpu.VMEM((heads * R, 128), F32),
            pltpu.VMEM((n * R, F), F32),
            pltpu.VMEM((n * R, F), F32),
            pltpu.VMEM(q_latent.shape, BF),
            pltpu.VMEM(cache_latent.shape, BF),
            pltpu.VMEM(cache_rope.shape, BF),
            pltpu.VMEM(q_latent.shape, BF),
            dma((3,)),
            dma((3,)),
            dma,
            dma((2, chips, pa)),
            dma((chips, pa)),
            dma((2, Z, pa)),
            dma((chips,)),
            dma((chips,)),
            dma((2, chips, pr)),
            dma((Z, pr)),
            dma((chips,)),
            dma((chips,)),
            dma((side, 2, pr)),
            dma((side, pr)),
            dma((Z, pr)),
        ],
        compiler_params=pltpu.CompilerParams(
            collective_id=0, has_side_effects=True, vmem_limit_bytes=60 << 20
        ),
        cost_estimate=pl.CostEstimate(flops=3 * 10**9, bytes_accessed=13 * 10**6, transcendentals=300000),
    )(
        normed, expert_ids.T, gate_levels.T, lengths, placement, w_gate, w_up, w_down,
        q_latent, q_rope, cache_latent, cache_rope,
    )


def grid_body(
    n,
    normed_hbm, ids_hbm, lev_hbm, len_hbm, place_hbm, wg_hbm, wu_hbm, wd_hbm,
    ql_hbm, qr_hbm, cl_hbm, cr_hbm,
    moe_ref, att_ref,
    xs, acc, rc, r1, r2, r3, rf, wg, wu, wd, own, ids, lev, qr, rq, ql, cl, cr, lens, place,
    in_sem, w_sem,
    ag_ss, agc_ss, agf_ss, ag_rs, agc_rs, rs_ss, rs_rs, far_ss, far_rs,
):
    Z, Y, X = chip_grid(n)
    plane = Y * X
    R, D = own.shape
    W = D + EXTRA
    F = wg.shape[1]
    top = ids.shape[0]
    me = lax.axis_index("expert")
    c = me % 2
    chip = me // 2
    z = chip // plane
    y = (chip % plane) // X
    x = chip % X
    pair = z // 2
    here = (z % 2, y, x)
    steps = (2 * plane, 2 * X, 2)
    peers = [me + s * (1 - 2 * v) for s, v in zip(steps, here)]
    peer_c = 2 * chip + 1 - c
    peer_f = me + 2 * plane * ((z + 2) % Z - z)

    def group(q):
        return (pair + q) % 2

    def order(p):
        return tuple((1 + p + k) % 3 for k in range(3))

    def spot(flips):
        return tuple(1 - v if e in flips else v for e, v in enumerate(here))

    barrier = pltpu.get_barrier_semaphore()
    for dev in (peer_c, *peers, peer_f):
        pl.semaphore_signal(barrier, inc=1, device_id={"expert": dev})

    loads = [
        pltpu.make_async_copy(src, dst, in_sem.at[k])
        for k, (src, dst) in enumerate((
            (normed_hbm, own), (ids_hbm, ids), (lev_hbm, lev), (len_hbm, lens), (place_hbm, place),
            (qr_hbm, qr), (ql_hbm, ql), (cl_hbm, cl), (cr_hbm, cr),
        ))
    ]
    for load in loads:
        load.start()
    weights = [
        pltpu.make_async_copy(src.at[0], dst, w_sem.at[k])
        for k, (src, dst) in enumerate(((wg_hbm, wg), (wu_hbm, wu), (wd_hbm, wd)))
    ]
    for load in weights:
        load.start()
    for load in loads[:3]:
        load.wait()

    base = (c, pair, *here, slice(None))
    xs[(*base, pl.ds(0, D))] = own[...]
    lane = lax.broadcasted_iota(jnp.int32, (R, EXTRA), 1)
    same = lax.broadcasted_iota(jnp.int32, (R, R), 0) == lax.broadcasted_iota(jnp.int32, (R, R), 1)

    def column(ref, k):
        row = jnp.broadcast_to(ref[k : k + 1, :].astype(F32), (R, R))
        return jnp.sum(jnp.where(same, row, 0.0), axis=1, keepdims=True)

    tail = jnp.zeros((R, EXTRA), F32)
    for k in range(top):
        tail = jnp.where(lane == k, column(ids, k), tail)
        tail = jnp.where(lane == top + k, column(lev, k), tail)
    xs[(*base, pl.ds(D, EXTRA))] = tail.astype(BF)

    pl.semaphore_wait(barrier, 5)

    wa = W // 3

    def piece(p):
        return pl.ds(p * wa, wa)

    def gather(q, p, flips, level):
        e = order(p)[level]
        j = spot(flips)
        part = xs.at[(c, group(q), *j, slice(None), piece(p))]
        return pltpu.make_async_remote_copy(
            part, part, ag_ss.at[q, p, level], ag_rs.at[(q, *j, p)], device_id={"expert": peers[e]}
        )

    def last(p, flips):
        return max(order(p).index(e) for e in flips)

    def got(q, p, flips):
        gather(q, p, flips, 0).wait_recv()

    def to_far_block(p):
        part = xs.at[(*base, piece(p))]
        return pltpu.make_async_remote_copy(
            part, part, agf_ss, ag_rs.at[(1, *here, p)], device_id={"expert": peer_f}
        )

    def core_block(q, j, cc):
        part = xs.at[(cc, group(q), *j)]
        return pltpu.make_async_remote_copy(
            part, part, agc_ss, agc_rs.at[(q, *j)], device_id={"expert": peer_c}
        )

    def subsets(level):
        return [tuple(k for k in range(level) if m >> k & 1) + (level,) for m in range(1 << level)]

    def own_along(q, level):
        for p in range(3):
            gather(q, p, (), level).start()

    def stage(q, level):
        for p in range(3):
            for ks in subsets(level):
                flips = tuple(order(p)[k] for k in ks)
                got(q, p, flips)
                for later in range(level + 1, 3):
                    gather(q, p, flips, later).start()

    def cross(q):
        for flips in ((0,), (1,), (2,), (0, 1), (0, 2), (1, 2), (0, 1, 2)):
            for p in range(3):
                if last(p, flips) == 2:
                    got(q, p, flips)
            core_block(q, spot(flips), c).start()

    def own_core(q):
        core_block(q, here, c).start()

    def far_in():
        for p in range(3):
            got(1, p, ())

    def gathered(q):
        for m in range(8):
            core_block(q, (m // 4, m // 2 % 2, m % 2), 1 - c).wait_recv()

    def far_out():
        for p in range(3):
            to_far_block(p).start()

    def prepare():
        for load in loads[3:]:
            load.wait()
        queries = qr[...].astype(F32)
        for h in range(heads):
            rq[h * R : (h + 1) * R, :rope] = queries[:, h * rope : (h + 1) * rope]

    heads, rope = ql.shape[1], cr.shape[1]
    lmax = cl.shape[1]

    def attend(t):
        keys = cl[t]
        rope_q = rq[pl.ds(t, heads, stride=R), :rope].astype(BF)
        s = lax.dot_general(ql[t], keys, (((1,), (1,)), ((), ())), preferred_element_type=F32)
        s = s + jnp.dot(rope_q, cr[t], preferred_element_type=F32)
        s = s * score_scale
        seen = lax.broadcasted_iota(jnp.int32, (heads, lmax), 1) < lens[t]
        s = jnp.where(seen, s, -1e30)
        e = jnp.where(seen, jnp.exp(s - jnp.max(s, axis=-1, keepdims=True)), 0.0)
        p = (e / jnp.sum(e, axis=-1, keepdims=True)).astype(BF)
        att_ref[t] = jnp.dot(p, keys, preferred_element_type=F32).astype(BF)

    rows = 16 * R
    tiles = D // 128
    ends = [128 * (tiles * k // 3) for k in range(4)]

    def cols(p):
        return pl.ds(ends[p], ends[p + 1] - ends[p])

    def part_of(fixed):
        return tuple(fixed.get(e, slice(None)) for e in range(3))

    def scatter_order(p):
        return tuple((p + k) % 3 for k in range(3))

    def kept(p, level, flip):
        axes = scatter_order(p)
        fixed = {e: here[e] for e in axes[:level]}
        if level < 3:
            fixed[axes[level]] = 1 - here[axes[level]] if flip else here[axes[level]]
        return fixed

    landing = (r1, r2, r3)

    def to_core(q, p):
        g = group(q)
        return pltpu.make_async_remote_copy(
            acc.at[1 - c, g, :, :, :, :, cols(p)], rc.at[g, :, :, :, :, cols(p)],
            rs_ss.at[q, p, 3], rs_rs.at[q, p, 3], device_id={"expert": peer_c},
        )

    def scatter(q, p, level):
        g = group(q)
        e = scatter_order(p)[level]
        src = acc.at[(c, g, *part_of(kept(p, level, True)), slice(None), cols(p))]
        dst = landing[level].at[(g,) + (slice(None),) * (2 - level) + (slice(None), cols(p))]
        return pltpu.make_async_remote_copy(
            src, dst, rs_ss.at[q, p, level], rs_rs.at[q, p, level], device_id={"expert": peers[e]}
        )

    def to_far(p):
        return pltpu.make_async_remote_copy(
            acc.at[(c, group(1), *here, slice(None), cols(p))], rf.at[:, cols(p)],
            far_ss.at[p], far_rs.at[p], device_id={"expert": peer_f},
        )

    def total_of(q, p, fixed, levels):
        g, cp = group(q), cols(p)
        axes = scatter_order(p)
        j = part_of(fixed)
        terms = [acc[(c, g, *j, slice(None), cp)], rc[(g, *j, slice(None), cp)]]
        for level in range(levels):
            rest = [e for e in range(3) if e not in axes[: level + 1]]
            terms.append(landing[level][(g, *(j[e] for e in rest), slice(None), cp)])
        return functools.reduce(lambda u, v: u + v, [t.astype(F32) for t in terms])

    def send(q, p, level):
        (to_core(q, p) if level == 0 else scatter(q, p, level - 1)).wait_recv()
        fixed = kept(p, level, True)
        acc[(c, group(q), *part_of(fixed), slice(None), cols(p))] = total_of(q, p, fixed, level).astype(BF)
        scatter(q, p, level).start()

    def send_far(p):
        scatter(1, p, 2).wait_recv()
        acc[(c, group(1), *here, slice(None), cols(p))] = total_of(1, p, kept(p, 3, False), 3).astype(BF)
        to_far(p).start()

    def finish(p):
        scatter(0, p, 2).wait_recv()
        to_far(p).wait_recv()
        moe_ref[:, cols(p)] = (total_of(0, p, kept(p, 3, False), 3) + rf[:, cols(p)].astype(F32)).astype(BF)

    kc = D // 2

    def compute(q):
        gq = group(q)
        g = jnp.zeros((rows, F), F32)
        u = jnp.zeros((rows, F), F32)
        for k in range(D // kc):
            ks = pl.ds(k * kc, kc)
            xk = xs[:, gq, :, :, :, :, ks].astype(F32).reshape(rows, kc).astype(BF)
            g += jnp.dot(xk, wg[ks, :], preferred_element_type=F32)
            u += jnp.dot(xk, wu[ks, :], preferred_element_type=F32)
        hidden = (g / (1.0 + jnp.exp(-g)) * u).astype(BF)
        mine = place[me].astype(F32)
        info = xs[:, gq, :, :, :, :, pl.ds(D, EXTRA)].astype(F32).reshape(rows, EXTRA)
        levels = [info[:, top + k : top + k + 1] for k in range(top)]
        total = functools.reduce(lambda p, q: p + q, levels)
        coef = jnp.zeros((rows, 1), F32)
        for k in range(top):
            coef = coef + jnp.where(info[:, k : k + 1] == mine, route_scale * levels[k] / total, 0.0)
        for p in range(3):
            width = ends[p + 1] - ends[p]
            out = jnp.dot(hidden, wd[:, cols(p)], preferred_element_type=F32).astype(BF).astype(F32)
            acc[:, gq, :, :, :, :, cols(p)] = (out * coef).reshape(2, 2, 2, 2, R, width).astype(BF)
            to_core(q, p).start()

    def weights_in():
        for load in weights:
            load.wait()

    def sends(q, level):
        for p in range(3):
            send(q, p, level)

    own_along(0, 0)
    far_out()
    own_along(0, 1)
    own_along(0, 2)
    own_core(0)
    prepare()
    attend(0)
    attend(1)
    attend(2)
    stage(0, 0)
    far_in()
    own_along(1, 0)
    stage(0, 1)
    own_along(1, 1)
    own_along(1, 2)
    own_core(1)
    attend(3)
    attend(4)
    cross(0)
    attend(5)
    stage(1, 0)
    attend(6)
    weights_in()
    gathered(0)
    compute(0)
    stage(1, 1)
    attend(7)
    sends(0, 0)
    cross(1)
    gathered(1)
    compute(1)
    sends(1, 0)
    sends(0, 1)
    sends(1, 1)
    sends(0, 2)
    sends(1, 2)
    for p in range(3):
        send_far(p)
    for p in range(3):
        finish(p)

    for q in range(2):
        for p in range(3):
            one = xs.at[c, 0, 0, 0, 0, :, piece(p)]
            two = xs.at[c, 0, 0, 0, :, :, piece(p)]
            four = xs.at[c, 0, 0, :, :, :, piece(p)]
            for level, part in enumerate((one, two, four)):
                pltpu.make_async_copy(part, part, ag_ss.at[q, p, level]).wait()
    pltpu.make_async_copy(xs.at[base], xs.at[base], agf_ss).wait()
    pltpu.make_async_copy(xs.at[c], xs.at[c], agc_ss).wait()
    for p in range(3):
        for q in range(2):
            to_core(q, p).wait_send()
            for level in range(3):
                scatter(q, p, level).wait_send()
        to_far(p).wait_send()


def on_grid(
    normed, expert_ids, gate_levels, placement, w_gate, w_up, w_down,
    q_latent, q_rope, cache_latent, cache_rope, lengths,
):
    n = lax.axis_size("expert")
    R, D = normed.shape
    F = w_gate.shape[2]
    heads, top = q_latent.shape[1], expert_ids.shape[1]
    vmem = pl.BlockSpec(memory_space=pltpu.VMEM)
    hbm = pl.BlockSpec(memory_space=pl.ANY)
    dma = pltpu.SemaphoreType.DMA
    return pl.pallas_call(
        functools.partial(grid_body, n),
        out_shape=(pltpu.VMEM((R, D), BF), pltpu.VMEM(q_latent.shape, BF)),
        in_specs=[hbm] * 12,
        out_specs=(vmem, vmem),
        scratch_shapes=[
            pltpu.VMEM((2, 2, 2, 2, 2, R, D + EXTRA), BF),
            pltpu.VMEM((2, 2, 2, 2, 2, R, D), BF),
            pltpu.VMEM((2, 2, 2, 2, R, D), BF),
            pltpu.VMEM((2, 2, 2, R, D), BF),
            pltpu.VMEM((2, 2, R, D), BF),
            pltpu.VMEM((2, R, D), BF),
            pltpu.VMEM((R, D), BF),
            pltpu.VMEM((D, F), BF),
            pltpu.VMEM((D, F), BF),
            pltpu.VMEM((F, D), BF),
            pltpu.VMEM((R, D), BF),
            pltpu.VMEM((top, R), jnp.int32),
            pltpu.VMEM((top, R), jnp.int32),
            pltpu.VMEM(q_rope.shape, BF),
            pltpu.VMEM((heads * R, 128), F32),
            pltpu.VMEM(q_latent.shape, BF),
            pltpu.VMEM(cache_latent.shape, BF),
            pltpu.VMEM(cache_rope.shape, BF),
            pltpu.SMEM((R,), jnp.int32),
            pltpu.SMEM((n,), jnp.int32),
            dma((9,)),
            dma((3,)),
            dma((2, 3, 3)),
            dma,
            dma,
            dma((2, 2, 2, 2, 3)),
            dma((2, 2, 2, 2)),
            dma((2, 3, 4)),
            dma((2, 3, 4)),
            dma((3,)),
            dma((3,)),
        ],
        compiler_params=pltpu.CompilerParams(
            collective_id=0, has_side_effects=True, vmem_limit_bytes=60 << 20
        ),
        cost_estimate=pl.CostEstimate(flops=3 * 10**9, bytes_accessed=13 * 10**6, transcendentals=300000),
    )(
        normed, expert_ids.T, gate_levels.T, lengths, placement, w_gate, w_up, w_down,
        q_latent, q_rope, cache_latent, cache_rope,
    )


def per_device(*args):
    n = lax.axis_size("expert")
    Z, Y, X = chip_grid(n)
    return on_grid(*args) if Y * X > 1 else on_line(*args)


def solution(mesh):
    rows = ("groups", "expert")
    in_specs = (
        P(rows, None), P(rows, None), P(rows, None), P(),
        P("expert", None, None), P("expert", None, None), P("expert", None, None),
        P(rows, None, None), P(rows, None), P(rows, None, None), P(rows, None, None), P(rows),
    )
    out_specs = (P(rows, None), P(rows, None, None))
    return jax.shard_map(
        per_device, mesh=mesh, in_specs=in_specs, out_specs=out_specs, check_vma=False
    )
```

```python
import functools

import jax
import jax.numpy as jnp
from jax import lax
from jax.experimental import pallas as pl
from jax.experimental.pallas import tpu as pltpu
from jax.sharding import PartitionSpec as P

score_scale = 192.0 ** (-0.5)
route_scale = 2.5
BF, F32 = jnp.bfloat16, jnp.float32
EXTRA = 128
PA, PR = 3, 2
SIDE_A, SIDE_B = range(2)


def chip_grid(n):
    return (4, 2, 2) if n == 32 else (n // 2, 1, 1)


def parts(cols, most):
    return max(p for p in range(1, most + 1) if cols % (128 * p) == 0)


def line_body(
    n,
    normed_ref, ids_ref, lev_ref, len_ref, place_ref, wg_hbm, wu_hbm, wd_hbm,
    ql_hbm, qr_ref, cl_hbm, cr_hbm,
    moe_ref, att_hbm,
    xs, acc, rc, rb, ra, rz, wg, wu, wd, h3, cf, rq, gacc, uacc, ql_ref, cl_ref, cr_ref, att_ref,
    w_sem, in_sem, out_sem, ag_ss, ag_rs, agz_ss, agc_ss, agc_rs, rs_ss, rsz_ss, rsc_ss, rc_s, rb_s, ra_s, rz_s,
):
    Z, Y, X = chip_grid(n)
    plane = Y * X
    planar = plane > 1
    chips = n // 2
    R, D = normed_ref.shape
    F = wg.shape[1]
    top = ids_ref.shape[0]
    me = lax.axis_index("expert")
    c = me % 2
    chip = me // 2
    z = chip // plane
    y = (chip % plane) // X
    x = chip % X
    a = x * (1 - c) + y * c
    b = y * (1 - c) + x * c
    sa = (1 - c) + X * c
    sb = X * (1 - c) + c
    peer_a = me + 2 * (1 - 2 * a) * sa
    peer_b = me + 2 * (1 - 2 * b) * sb
    peer_c = 2 * chip + 1 - c

    def at(zz, aa, bb):
        if planar:
            return zz * plane + aa * sa + bb * sb
        return zz

    barrier = pltpu.get_barrier_semaphore()

    def greet(dev):
        pl.semaphore_signal(barrier, inc=1, device_id={"expert": dev})

    greet(peer_c)
    if planar:
        greet(peer_a)
        greet(peer_b)
    for d in range(1, Z):
        greet(me + 2 * plane * ((z + d) % Z - z))
    for src, dst, s in ((wg_hbm, wg, 0), (wu_hbm, wu, 1), (wd_hbm, wd, 2)):
        pltpu.make_async_copy(src.at[0], dst, w_sem.at[s]).start()

    for k, (src, dst) in enumerate(((ql_hbm, ql_ref), (cl_hbm, cl_ref), (cr_hbm, cr_ref))):
        pltpu.make_async_copy(src, dst, in_sem.at[k]).start()

    xs[chip, c, :, pl.ds(0, D)] = normed_ref[...]
    lane = lax.broadcasted_iota(jnp.int32, (R, EXTRA), 1)
    same = lax.broadcasted_iota(jnp.int32, (R, R), 0) == lax.broadcasted_iota(jnp.int32, (R, R), 1)

    def column(ref, k):
        row = jnp.broadcast_to(ref[k : k + 1, :].astype(F32), (R, R))
        return jnp.sum(jnp.where(same, row, 0.0), axis=1, keepdims=True)

    tail = jnp.zeros((R, EXTRA), F32)
    for k in range(top):
        tail = jnp.where(lane == k, column(ids_ref, k), tail)
        tail = jnp.where(lane == top + k, column(lev_ref, k), tail)
    xs[chip, c, :, pl.ds(D, EXTRA)] = tail.astype(BF)

    pl.semaphore_wait(barrier, Z - 1 + (3 if planar else 1))

    pa = ag_rs.shape[1]
    wa = (D + EXTRA) // pa

    def ag(i, p, way, dev):
        part = xs.at[i, c, :, pl.ds(p * wa, wa)]
        return pltpu.make_async_remote_copy(
            part, part, ag_ss.at[way, i, p], ag_rs.at[i, p], device_id={"expert": dev}
        )

    def ag_core(i, cc):
        return pltpu.make_async_remote_copy(
            xs.at[i, cc], xs.at[i, cc], agc_ss.at[i], agc_rs.at[i], device_id={"expert": peer_c}
        )

    def got(i, p):
        ag(i, p, SIDE_A, peer_a).wait_recv()

    def ag_z(zz, p, way, dev):
        i = at(zz, a, b)
        part = xs.at[i, c, :, pl.ds(p * wa, wa)]
        return pltpu.make_async_remote_copy(
            part, part, agz_ss.at[way, zz, p], ag_rs.at[i, p], device_id={"expert": dev}
        )

    def go_up(zz, p):
        pl.when(z < Z - 1)(lambda: ag_z(zz, p, 0, me + 2 * plane).start())

    def go_down(zz, p):
        pl.when(z > 0)(lambda: ag_z(zz, p, 1, me - 2 * plane).start())

    def share(zz, wait, *onward):
        i = at(zz, a, b)
        for p in range(pa):
            if wait:
                got(i, p)
            for step in onward:
                step(zz, p)
            if planar:
                ag(i, p, SIDE_A, peer_a).start()
                ag(i, p, SIDE_B, peer_b).start()
        ag_core(i, c).start()

    def column_dev(zz):
        return me + 2 * plane * (zz - z)

    share(z, False, go_up, go_down)

    qr = qr_ref[...].astype(F32)
    heads, rope = ql_ref.shape[1], cr_ref.shape[1]
    for h in range(heads):
        rq[h * R : (h + 1) * R, :rope] = qr[:, h * rope : (h + 1) * rope]

    lmax = cl_ref.shape[1]
    for k, (src, dst) in enumerate(((ql_hbm, ql_ref), (cl_hbm, cl_ref), (cr_hbm, cr_ref))):
        pltpu.make_async_copy(src, dst, in_sem.at[k]).wait()

    def attend(t):
        keys = cl_ref[t]
        rope_q = rq[pl.ds(t, heads, stride=R), :rope].astype(BF)
        s = lax.dot_general(ql_ref[t], keys, (((1,), (1,)), ((), ())), preferred_element_type=F32)
        s = s + jnp.dot(rope_q, cr_ref[t], preferred_element_type=F32)
        s = s * score_scale
        seen = lax.broadcasted_iota(jnp.int32, (heads, lmax), 1) < len_ref[t]
        s = jnp.where(seen, s, -1e30)
        e = jnp.where(seen, jnp.exp(s - jnp.max(s, axis=-1, keepdims=True)), 0.0)
        p = (e / jnp.sum(e, axis=-1, keepdims=True)).astype(BF)
        att_ref[t] = jnp.dot(p, keys, preferred_element_type=F32).astype(BF)

    def from_a(zz):
        i = at(zz, 1 - a, b)
        for p in range(pa):
            got(i, p)
            ag(i, p, SIDE_B, peer_b).start()
        ag_core(i, c).start()

    if planar:
        from_a(z)

    def z_step(d, carry):
        pl.when(z - d >= 0)(lambda: share(z - d, True, go_up))
        pl.when(z + d < Z)(lambda: share(z + d, True, go_down))
        if planar:
            pl.when(z - d >= 0)(lambda: from_a(z - d))
            pl.when(z + d < Z)(lambda: from_a(z + d))
        return carry

    lax.fori_loop(1, Z, z_step, 0)

    if planar:
        def from_b(k, carry):
            attend(k)
            i = at((z + k // 2) % Z, k % 2, 1 - b)
            for p in range(pa):
                got(i, p)
            ag_core(i, c).start()
            return carry

        lax.fori_loop(0, 2 * Z, from_b, 0)
        first = min(2 * Z, R)
    else:
        first = 0
    for t in range(first, R):
        attend(t)

    pltpu.make_async_copy(att_ref, att_hbm, out_sem).start()

    def from_core(i, carry):
        ag_core(i, 1 - c).wait_recv()
        return carry

    lax.fori_loop(0, chips, from_core, 0)

    for src, dst, s in ((wg_hbm, wg, 0), (wu_hbm, wu, 1), (wd_hbm, wd, 2)):
        pltpu.make_async_copy(src.at[0], dst, w_sem.at[s]).wait()
    rows = n * R
    kc = 3584
    gacc[...] = jnp.zeros_like(gacc)
    uacc[...] = jnp.zeros_like(uacc)

    def k_step(k, carry):
        ks = pl.ds(pl.multiple_of(k * kc, kc), kc)
        xk = xs[:, :, :, ks].astype(F32).reshape(rows, kc).astype(BF)
        gacc[...] += jnp.dot(xk, wg[ks, :], preferred_element_type=F32)
        uacc[...] += jnp.dot(xk, wu[ks, :], preferred_element_type=F32)
        return carry

    lax.fori_loop(0, D // kc, k_step, 0)
    g = gacc[...]
    hidden = (g / (1.0 + jnp.exp(-g)) * uacc[...]).astype(BF)
    h3[...] = hidden.astype(F32).reshape(chips, 2, R, F)

    mine = place_ref[me].astype(F32)
    info = xs[:, :, :, pl.ds(D, EXTRA)].astype(F32).reshape(rows, EXTRA)
    levels = [info[:, top + k : top + k + 1] for k in range(top)]
    total = functools.reduce(lambda p, q: p + q, levels)
    coef = jnp.zeros((rows, 1), F32)
    for k in range(top):
        coef = coef + jnp.where(info[:, k : k + 1] == mine, route_scale * levels[k] / total, 0.0)
    cf[...] = jnp.broadcast_to(coef, (rows, EXTRA)).reshape(chips, 2, R, EXTRA)

    nc = 1792

    def down_half(cc):
        hh = h3[:, cc].reshape(chips * R, F).astype(BF)
        scale = cf[:, cc].reshape(chips * R, EXTRA)[:, :1]

        def n_step(k, carry):
            ns = pl.ds(pl.multiple_of(k * nc, nc), nc)
            p = jnp.dot(hh, wd[:, ns], preferred_element_type=F32).astype(BF).astype(F32)
            acc[:, cc, :, ns] = (p * scale).reshape(chips, R, nc).astype(BF)
            return carry

        lax.fori_loop(0, D // nc, n_step, 0)

    pr = rz_s.shape[1]
    wr = D // pr

    def cols(p):
        return pl.ds(p * wr, wr)

    def to_core(i):
        return pltpu.make_async_remote_copy(
            acc.at[i, 1 - c], rc.at[i], rsc_ss.at[i], rc_s.at[i], device_id={"expert": peer_c}
        )

    def to_b(zz, aa, p):
        i = at(zz, aa, 1 - b)
        return pltpu.make_async_remote_copy(
            acc.at[i, c, :, cols(p)], rb.at[zz, aa, :, cols(p)], rs_ss.at[SIDE_B, i, p],
            rb_s.at[zz, aa, p], device_id={"expert": peer_b},
        )

    def to_a(zz, p):
        i = at(zz, 1 - a, b)
        return pltpu.make_async_remote_copy(
            acc.at[i, c, :, cols(p)], ra.at[zz, :, cols(p)], rs_ss.at[SIDE_A, i, p],
            ra_s.at[zz, p], device_id={"expert": peer_a},
        )

    def to_z(zz, p):
        return pltpu.make_async_remote_copy(
            acc.at[at(zz, a, b), c, :, cols(p)], rz.at[z, :, cols(p)], rsz_ss.at[zz, p],
            rz_s.at[z, p], device_id={"expert": column_dev(zz)},
        )

    def from_z(zz, p):
        return pltpu.make_async_remote_copy(
            acc.at[chip, c, :, cols(p)], rz.at[zz, :, cols(p)], rsz_ss.at[zz, p],
            rz_s.at[zz, p], device_id={"expert": column_dev(zz)},
        )

    down_half(1 - c)

    def far(k):
        return (z + 1 + k) % Z

    def core_send(k, carry):
        if planar:
            q = k % (chips // 2)
            zz, other = far(q // 2), 1 - q % 2
            away = 1 - k // (chips // 2)
            aa = (1 - 2 * a) * away + a
            bb = (1 - 2 * b) * other + b
            to_core(at(zz, aa, bb)).start()
        else:
            to_core(far(k)).start()
        return carry

    lax.fori_loop(0, chips, core_send, 0)
    down_half(c)

    def plus(*terms):
        return functools.reduce(lambda p, q: p + q, [t.astype(F32) for t in terms])

    if planar:
        def b_send(k, carry):
            zz = far(k // 2)
            aa = (1 - 2 * a) * (1 - k % 2) + a
            i = at(zz, aa, 1 - b)
            to_core(i).wait_recv()
            acc[i, c] = plus(acc[i, c], rc[i]).astype(BF)
            for p in range(pr):
                to_b(zz, aa, p).start()
            return carry

        lax.fori_loop(0, 2 * Z, b_send, 0)

        def a_send(k):
            zz = far(k)
            i = at(zz, 1 - a, b)
            to_core(i).wait_recv()
            for p in range(pr):
                to_b(zz, 1 - a, p).wait_recv()
                cp = cols(p)
                acc[i, c, :, cp] = plus(acc[i, c, :, cp], rc[i, :, cp], rb[zz, 1 - a, :, cp]).astype(BF)
                to_a(zz, p).start()

        a_send(0)

    def column_sum(zz, p):
        i = at(zz, a, b)
        cp = cols(p)
        if planar:
            to_b(zz, a, p).wait_recv()
            to_a(zz, p).wait_recv()
            return plus(acc[i, c, :, cp], rc[i, :, cp], rb[zz, a, :, cp], ra[zz, :, cp])
        return plus(acc[i, c, :, cp], rc[i, :, cp])

    def z_send(k, carry):
        if planar:
            a_send(k + 1)
        zz = far(k)
        to_core(at(zz, a, b)).wait_recv()
        for p in range(pr):
            acc[at(zz, a, b), c, :, cols(p)] = column_sum(zz, p).astype(BF)
            to_z(zz, p).start()
        return carry

    lax.fori_loop(0, Z - 1, z_send, 0)
    to_core(chip).wait_recv()
    for p in range(pr):
        result = column_sum(z, p)
        for d in range(1, Z):
            zz = (z + d) % Z
            from_z(zz, p).wait_recv()
            result = result + rz[zz, :, cols(p)].astype(F32)
        moe_ref[:, cols(p)] = result.astype(BF)

    pltpu.make_async_copy(att_ref, att_hbm, out_sem).wait()

    def core_done(i, carry):
        ag_core(i, c).wait_send()
        to_core(i).wait_send()
        return carry

    lax.fori_loop(0, chips, core_done, 0)

    def z_done(zz, carry):
        i = at(zz, a, b)

        @pl.when(zz != z)
        def _():
            for p in range(pr):
                to_z(zz, p).wait_send()

        for p in range(pa):
            pl.when((zz <= z) & (z < Z - 1))(lambda: ag_z(zz, p, 0, me + 2 * plane).wait_send())
            pl.when((zz >= z) & (z > 0))(lambda: ag_z(zz, p, 1, me - 2 * plane).wait_send())
        if planar:
            for p in range(pa):
                ag(i, p, SIDE_A, peer_a).wait_send()
                for aa in range(2):
                    ag(at(zz, aa, b), p, SIDE_B, peer_b).wait_send()
            for p in range(pr):
                to_a(zz, p).wait_send()
                for aa in range(2):
                    to_b(zz, aa, p).wait_send()
        return carry

    lax.fori_loop(0, Z, z_done, 0)


def on_line(
    normed, expert_ids, gate_levels, placement, w_gate, w_up, w_down,
    q_latent, q_rope, cache_latent, cache_rope, lengths,
):
    n = lax.axis_size("expert")
    Z, Y, X = chip_grid(n)
    chips = n // 2
    R, D = normed.shape
    F = w_gate.shape[2]
    heads = q_latent.shape[1]
    vmem = pl.BlockSpec(memory_space=pltpu.VMEM)
    smem = pl.BlockSpec(memory_space=pltpu.SMEM)
    hbm = pl.BlockSpec(memory_space=pl.ANY)
    dma = pltpu.SemaphoreType.DMA
    side = Z if Y * X > 1 else 1
    pa, pr = parts(D + EXTRA, PA), parts(D, PR)
    return pl.pallas_call(
        functools.partial(line_body, n),
        out_shape=(
            jax.ShapeDtypeStruct((R, D), BF),
            jax.ShapeDtypeStruct(q_latent.shape, BF),
        ),
        in_specs=[vmem, vmem, vmem, smem, smem, hbm, hbm, hbm, hbm, vmem, hbm, hbm],
        out_specs=(vmem, hbm),
        scratch_shapes=[
            pltpu.VMEM((chips, 2, R, D + EXTRA), BF),
            pltpu.VMEM((chips, 2, R, D), BF),
            pltpu.VMEM((chips, R, D), BF),
            pltpu.VMEM((side, 2, R, D), BF),
            pltpu.VMEM((side, R, D), BF),
            pltpu.VMEM((Z, R, D), BF),
            pltpu.VMEM((D, F), BF),
            pltpu.VMEM((D, F), BF),
            pltpu.VMEM((F, D), BF),
            pltpu.VMEM((chips, 2, R, F), F32),
            pltpu.VMEM((chips, 2, R, EXTRA), F32),
            pltpu.VMEM((heads * R, 128), F32),
            pltpu.VMEM((n * R, F), F32),
            pltpu.VMEM((n * R, F), F32),
            pltpu.VMEM(q_latent.shape, BF),
            pltpu.VMEM(cache_latent.shape, BF),
            pltpu.VMEM(cache_rope.shape, BF),
            pltpu.VMEM(q_latent.shape, BF),
            dma((3,)),
            dma((3,)),
            dma,
            dma((2, chips, pa)),
            dma((chips, pa)),
            dma((2, Z, pa)),
            dma((chips,)),
            dma((chips,)),
            dma((2, chips, pr)),
            dma((Z, pr)),
            dma((chips,)),
            dma((chips,)),
            dma((side, 2, pr)),
            dma((side, pr)),
            dma((Z, pr)),
        ],
        compiler_params=pltpu.CompilerParams(
            collective_id=0, has_side_effects=True, vmem_limit_bytes=60 << 20
        ),
        cost_estimate=pl.CostEstimate(flops=3 * 10**9, bytes_accessed=13 * 10**6, transcendentals=300000),
    )(
        normed, expert_ids.T, gate_levels.T, lengths, placement, w_gate, w_up, w_down,
        q_latent, q_rope, cache_latent, cache_rope,
    )


def grid_body(
    n,
    normed_hbm, ids_hbm, lev_hbm, len_hbm, place_hbm, wg_hbm, wu_hbm, wd_hbm,
    ql_hbm, qr_hbm, cl_hbm, cr_hbm,
    moe_ref, att_ref,
    xs, acc, rc, r1, r2, r3, rf, wg, wu, wd, own, ids, lev, qr, rq, ql, cl, cr, lens, place,
    in_sem, w_sem,
    ag_ss, agc_ss, agf_ss, ag_rs, agc_rs, rs_ss, rs_rs, far_ss, far_rs,
):
    Z, Y, X = chip_grid(n)
    plane = Y * X
    R, D = own.shape
    W = D + EXTRA
    F = wg.shape[1]
    top = ids.shape[0]
    me = lax.axis_index("expert")
    c = me % 2
    chip = me // 2
    z = chip // plane
    y = (chip % plane) // X
    x = chip % X
    pair = z // 2
    here = (z % 2, y, x)
    steps = (2 * plane, 2 * X, 2)
    peers = [me + s * (1 - 2 * v) for s, v in zip(steps, here)]
    peer_c = 2 * chip + 1 - c
    peer_f = me + 2 * plane * ((z + 2) % Z - z)

    def group(q):
        return (pair + q) % 2

    def order(p):
        return tuple((1 + p + k) % 3 for k in range(3))

    def spot(flips):
        return tuple(1 - v if e in flips else v for e, v in enumerate(here))

    barrier = pltpu.get_barrier_semaphore()
    for dev in (peer_c, *peers, peer_f):
        pl.semaphore_signal(barrier, inc=1, device_id={"expert": dev})

    loads = [
        pltpu.make_async_copy(src, dst, in_sem.at[k])
        for k, (src, dst) in enumerate((
            (normed_hbm, own), (ids_hbm, ids), (lev_hbm, lev), (len_hbm, lens), (place_hbm, place),
            (qr_hbm, qr), (ql_hbm, ql), (cl_hbm, cl), (cr_hbm, cr),
        ))
    ]
    for load in loads:
        load.start()
    weights = [
        pltpu.make_async_copy(src.at[0], dst, w_sem.at[k])
        for k, (src, dst) in enumerate(((wg_hbm, wg), (wu_hbm, wu), (wd_hbm, wd)))
    ]
    for load in weights:
        load.start()
    for load in loads[:3]:
        load.wait()

    base = (c, pair, *here, slice(None))
    xs[(*base, pl.ds(0, D))] = own[...]
    lane = lax.broadcasted_iota(jnp.int32, (R, EXTRA), 1)
    same = lax.broadcasted_iota(jnp.int32, (R, R), 0) == lax.broadcasted_iota(jnp.int32, (R, R), 1)

    def column(ref, k):
        row = jnp.broadcast_to(ref[k : k + 1, :].astype(F32), (R, R))
        return jnp.sum(jnp.where(same, row, 0.0), axis=1, keepdims=True)

    tail = jnp.zeros((R, EXTRA), F32)
    for k in range(top):
        tail = jnp.where(lane == k, column(ids, k), tail)
        tail = jnp.where(lane == top + k, column(lev, k), tail)
    xs[(*base, pl.ds(D, EXTRA))] = tail.astype(BF)

    pl.semaphore_wait(barrier, 5)

    wa = W // 3

    def piece(p):
        return pl.ds(p * wa, wa)

    def gather(q, p, flips, level):
        e = order(p)[level]
        j = spot(flips)
        part = xs.at[(c, group(q), *j, slice(None), piece(p))]
        return pltpu.make_async_remote_copy(
            part, part, ag_ss.at[q, p, level], ag_rs.at[(q, *j, p)], device_id={"expert": peers[e]}
        )

    def last(p, flips):
        return max(order(p).index(e) for e in flips)

    def got(q, p, flips):
        gather(q, p, flips, 0).wait_recv()

    def to_far_block(p):
        part = xs.at[(*base, piece(p))]
        return pltpu.make_async_remote_copy(
            part, part, agf_ss, ag_rs.at[(1, *here, p)], device_id={"expert": peer_f}
        )

    def core_block(q, j, cc):
        part = xs.at[(cc, group(q), *j)]
        return pltpu.make_async_remote_copy(
            part, part, agc_ss, agc_rs.at[(q, *j)], device_id={"expert": peer_c}
        )

    def subsets(level):
        return [tuple(k for k in range(level) if m >> k & 1) + (level,) for m in range(1 << level)]

    def own_along(q, level):
        for p in range(3):
            gather(q, p, (), level).start()

    def stage(q, level):
        for p in range(3):
            for ks in subsets(level):
                flips = tuple(order(p)[k] for k in ks)
                got(q, p, flips)
                for later in range(level + 1, 3):
                    gather(q, p, flips, later).start()

    def cross(q):
        for flips in ((0,), (1,), (2,), (0, 1), (0, 2), (1, 2), (0, 1, 2)):
            for p in range(3):
                if last(p, flips) == 2:
                    got(q, p, flips)
            core_block(q, spot(flips), c).start()

    def own_core(q):
        core_block(q, here, c).start()

    def far_in():
        for p in range(3):
            got(1, p, ())

    def gathered(q):
        for m in range(8):
            core_block(q, (m // 4, m // 2 % 2, m % 2), 1 - c).wait_recv()

    def far_out():
        for p in range(3):
            to_far_block(p).start()

    def prepare():
        for load in loads[3:]:
            load.wait()
        queries = qr[...].astype(F32)
        for h in range(heads):
            rq[h * R : (h + 1) * R, :rope] = queries[:, h * rope : (h + 1) * rope]

    heads, rope = ql.shape[1], cr.shape[1]
    lmax = cl.shape[1]

    def attend(t):
        keys = cl[t]
        rope_q = rq[pl.ds(t, heads, stride=R), :rope].astype(BF)
        s = lax.dot_general(ql[t], keys, (((1,), (1,)), ((), ())), preferred_element_type=F32)
        s = s + jnp.dot(rope_q, cr[t], preferred_element_type=F32)
        s = s * score_scale
        seen = lax.broadcasted_iota(jnp.int32, (heads, lmax), 1) < lens[t]
        s = jnp.where(seen, s, -1e30)
        e = jnp.where(seen, jnp.exp(s - jnp.max(s, axis=-1, keepdims=True)), 0.0)
        p = (e / jnp.sum(e, axis=-1, keepdims=True)).astype(BF)
        att_ref[t] = jnp.dot(p, keys, preferred_element_type=F32).astype(BF)

    rows = 16 * R
    tiles = D // 128
    ends = [128 * (tiles * k // 3) for k in range(4)]

    def cols(p):
        return pl.ds(ends[p], ends[p + 1] - ends[p])

    def part_of(fixed):
        return tuple(fixed.get(e, slice(None)) for e in range(3))

    def scatter_order(p):
        return tuple((p + k) % 3 for k in range(3))

    def kept(p, level, flip):
        axes = scatter_order(p)
        fixed = {e: here[e] for e in axes[:level]}
        if level < 3:
            fixed[axes[level]] = 1 - here[axes[level]] if flip else here[axes[level]]
        return fixed

    landing = (r1, r2, r3)

    def to_core(q, p):
        g = group(q)
        return pltpu.make_async_remote_copy(
            acc.at[1 - c, g, :, :, :, :, cols(p)], rc.at[g, :, :, :, :, cols(p)],
            rs_ss.at[q, p, 3], rs_rs.at[q, p, 3], device_id={"expert": peer_c},
        )

    def scatter(q, p, level):
        g = group(q)
        e = scatter_order(p)[level]
        src = acc.at[(c, g, *part_of(kept(p, level, True)), slice(None), cols(p))]
        dst = landing[level].at[(g,) + (slice(None),) * (2 - level) + (slice(None), cols(p))]
        return pltpu.make_async_remote_copy(
            src, dst, rs_ss.at[q, p, level], rs_rs.at[q, p, level], device_id={"expert": peers[e]}
        )

    def to_far(p):
        return pltpu.make_async_remote_copy(
            acc.at[(c, group(1), *here, slice(None), cols(p))], rf.at[:, cols(p)],
            far_ss.at[p], far_rs.at[p], device_id={"expert": peer_f},
        )

    def total_of(q, p, fixed, levels):
        g, cp = group(q), cols(p)
        axes = scatter_order(p)
        j = part_of(fixed)
        terms = [acc[(c, g, *j, slice(None), cp)], rc[(g, *j, slice(None), cp)]]
        for level in range(levels):
            rest = [e for e in range(3) if e not in axes[: level + 1]]
            terms.append(landing[level][(g, *(j[e] for e in rest), slice(None), cp)])
        return functools.reduce(lambda u, v: u + v, [t.astype(F32) for t in terms])

    def send(q, p, level):
        (to_core(q, p) if level == 0 else scatter(q, p, level - 1)).wait_recv()
        fixed = kept(p, level, True)
        acc[(c, group(q), *part_of(fixed), slice(None), cols(p))] = total_of(q, p, fixed, level).astype(BF)
        scatter(q, p, level).start()

    def send_far(p):
        scatter(1, p, 2).wait_recv()
        acc[(c, group(1), *here, slice(None), cols(p))] = total_of(1, p, kept(p, 3, False), 3).astype(BF)
        to_far(p).start()

    def finish(p):
        scatter(0, p, 2).wait_recv()
        to_far(p).wait_recv()
        moe_ref[:, cols(p)] = (total_of(0, p, kept(p, 3, False), 3) + rf[:, cols(p)].astype(F32)).astype(BF)

    kc = D // 2

    def compute(q):
        gq = group(q)
        g = jnp.zeros((rows, F), F32)
        u = jnp.zeros((rows, F), F32)
        for k in range(D // kc):
            ks = pl.ds(k * kc, kc)
            xk = xs[:, gq, :, :, :, :, ks].astype(F32).reshape(rows, kc).astype(BF)
            g += jnp.dot(xk, wg[ks, :], preferred_element_type=F32)
            u += jnp.dot(xk, wu[ks, :], preferred_element_type=F32)
        hidden = (g / (1.0 + jnp.exp(-g)) * u).astype(BF)
        mine = place[me].astype(F32)
        info = xs[:, gq, :, :, :, :, pl.ds(D, EXTRA)].astype(F32).reshape(rows, EXTRA)
        levels = [info[:, top + k : top + k + 1] for k in range(top)]
        total = functools.reduce(lambda p, q: p + q, levels)
        coef = jnp.zeros((rows, 1), F32)
        for k in range(top):
            coef = coef + jnp.where(info[:, k : k + 1] == mine, route_scale * levels[k] / total, 0.0)
        for p in range(3):
            width = ends[p + 1] - ends[p]
            out = jnp.dot(hidden, wd[:, cols(p)], preferred_element_type=F32).astype(BF).astype(F32)
            acc[:, gq, :, :, :, :, cols(p)] = (out * coef).reshape(2, 2, 2, 2, R, width).astype(BF)
            to_core(q, p).start()

    def weights_in():
        for load in weights:
            load.wait()

    def sends(q, level):
        for p in range(3):
            send(q, p, level)

    own_along(0, 0)
    far_out()
    own_along(0, 1)
    own_along(0, 2)
    own_core(0)
    prepare()
    attend(0)
    attend(1)
    attend(2)
    stage(0, 0)
    far_in()
    own_along(1, 0)
    stage(0, 1)
    own_along(1, 1)
    own_core(1)
    attend(3)
    attend(4)
    cross(0)
    own_along(1, 2)
    attend(5)
    stage(1, 0)
    attend(6)
    weights_in()
    gathered(0)
    compute(0)
    stage(1, 1)
    attend(7)
    sends(0, 0)
    cross(1)
    gathered(1)
    compute(1)
    sends(1, 0)
    sends(0, 1)
    sends(1, 1)
    sends(0, 2)
    sends(1, 2)
    for p in range(3):
        send_far(p)
    for p in range(3):
        finish(p)

    for q in range(2):
        for p in range(3):
            one = xs.at[c, 0, 0, 0, 0, :, piece(p)]
            two = xs.at[c, 0, 0, 0, :, :, piece(p)]
            four = xs.at[c, 0, 0, :, :, :, piece(p)]
            for level, part in enumerate((one, two, four)):
                pltpu.make_async_copy(part, part, ag_ss.at[q, p, level]).wait()
    pltpu.make_async_copy(xs.at[base], xs.at[base], agf_ss).wait()
    pltpu.make_async_copy(xs.at[c], xs.at[c], agc_ss).wait()
    for p in range(3):
        for q in range(2):
            to_core(q, p).wait_send()
            for level in range(3):
                scatter(q, p, level).wait_send()
        to_far(p).wait_send()


def on_grid(
    normed, expert_ids, gate_levels, placement, w_gate, w_up, w_down,
    q_latent, q_rope, cache_latent, cache_rope, lengths,
):
    n = lax.axis_size("expert")
    R, D = normed.shape
    F = w_gate.shape[2]
    heads, top = q_latent.shape[1], expert_ids.shape[1]
    vmem = pl.BlockSpec(memory_space=pltpu.VMEM)
    hbm = pl.BlockSpec(memory_space=pl.ANY)
    dma = pltpu.SemaphoreType.DMA
    return pl.pallas_call(
        functools.partial(grid_body, n),
        out_shape=(pltpu.VMEM((R, D), BF), pltpu.VMEM(q_latent.shape, BF)),
        in_specs=[hbm] * 12,
        out_specs=(vmem, vmem),
        scratch_shapes=[
            pltpu.VMEM((2, 2, 2, 2, 2, R, D + EXTRA), BF),
            pltpu.VMEM((2, 2, 2, 2, 2, R, D), BF),
            pltpu.VMEM((2, 2, 2, 2, R, D), BF),
            pltpu.VMEM((2, 2, 2, R, D), BF),
            pltpu.VMEM((2, 2, R, D), BF),
            pltpu.VMEM((2, R, D), BF),
            pltpu.VMEM((R, D), BF),
            pltpu.VMEM((D, F), BF),
            pltpu.VMEM((D, F), BF),
            pltpu.VMEM((F, D), BF),
            pltpu.VMEM((R, D), BF),
            pltpu.VMEM((top, R), jnp.int32),
            pltpu.VMEM((top, R), jnp.int32),
            pltpu.VMEM(q_rope.shape, BF),
            pltpu.VMEM((heads * R, 128), F32),
            pltpu.VMEM(q_latent.shape, BF),
            pltpu.VMEM(cache_latent.shape, BF),
            pltpu.VMEM(cache_rope.shape, BF),
            pltpu.SMEM((R,), jnp.int32),
            pltpu.SMEM((n,), jnp.int32),
            dma((9,)),
            dma((3,)),
            dma((2, 3, 3)),
            dma,
            dma,
            dma((2, 2, 2, 2, 3)),
            dma((2, 2, 2, 2)),
            dma((2, 3, 4)),
            dma((2, 3, 4)),
            dma((3,)),
            dma((3,)),
        ],
        compiler_params=pltpu.CompilerParams(
            collective_id=0, has_side_effects=True, vmem_limit_bytes=60 << 20
        ),
        cost_estimate=pl.CostEstimate(flops=3 * 10**9, bytes_accessed=13 * 10**6, transcendentals=300000),
    )(
        normed, expert_ids.T, gate_levels.T, lengths, placement, w_gate, w_up, w_down,
        q_latent, q_rope, cache_latent, cache_rope,
    )


def per_device(*args):
    n = lax.axis_size("expert")
    Z, Y, X = chip_grid(n)
    return on_grid(*args) if Y * X > 1 else on_line(*args)


def solution(mesh):
    rows = ("groups", "expert")
    in_specs = (
        P(rows, None), P(rows, None), P(rows, None), P(),
        P("expert", None, None), P("expert", None, None), P("expert", None, None),
        P(rows, None, None), P(rows, None), P(rows, None, None), P(rows, None, None), P(rows),
    )
    out_specs = (P(rows, None), P(rows, None, None))
    return jax.shard_map(
        per_device, mesh=mesh, in_specs=in_specs, out_specs=out_specs, check_vma=False
    )
```

```python
import functools

import jax
import jax.numpy as jnp
from jax import lax
from jax.experimental import pallas as pl
from jax.experimental.pallas import tpu as pltpu
from jax.sharding import PartitionSpec as P

score_scale = 192.0 ** (-0.5)
route_scale = 2.5
BF, F32 = jnp.bfloat16, jnp.float32
EXTRA = 128
PA, PR = 3, 2
SIDE_A, SIDE_B = range(2)


def chip_grid(n):
    return (4, 2, 2) if n == 32 else (n // 2, 1, 1)


def parts(cols, most):
    return max(p for p in range(1, most + 1) if cols % (128 * p) == 0)


def line_body(
    n,
    normed_ref, ids_ref, lev_ref, len_ref, place_ref, wg_hbm, wu_hbm, wd_hbm,
    ql_hbm, qr_ref, cl_hbm, cr_hbm,
    moe_ref, att_hbm,
    xs, acc, rc, rb, ra, rz, wg, wu, wd, h3, cf, rq, gacc, uacc, ql_ref, cl_ref, cr_ref, att_ref,
    w_sem, in_sem, out_sem, ag_ss, ag_rs, agz_ss, agc_ss, agc_rs, rs_ss, rsz_ss, rsc_ss, rc_s, rb_s, ra_s, rz_s,
):
    Z, Y, X = chip_grid(n)
    plane = Y * X
    planar = plane > 1
    chips = n // 2
    R, D = normed_ref.shape
    F = wg.shape[1]
    top = ids_ref.shape[0]
    me = lax.axis_index("expert")
    c = me % 2
    chip = me // 2
    z = chip // plane
    y = (chip % plane) // X
    x = chip % X
    a = x * (1 - c) + y * c
    b = y * (1 - c) + x * c
    sa = (1 - c) + X * c
    sb = X * (1 - c) + c
    peer_a = me + 2 * (1 - 2 * a) * sa
    peer_b = me + 2 * (1 - 2 * b) * sb
    peer_c = 2 * chip + 1 - c

    def at(zz, aa, bb):
        if planar:
            return zz * plane + aa * sa + bb * sb
        return zz

    barrier = pltpu.get_barrier_semaphore()

    def greet(dev):
        pl.semaphore_signal(barrier, inc=1, device_id={"expert": dev})

    greet(peer_c)
    if planar:
        greet(peer_a)
        greet(peer_b)
    for d in range(1, Z):
        greet(me + 2 * plane * ((z + d) % Z - z))
    for src, dst, s in ((wg_hbm, wg, 0), (wu_hbm, wu, 1), (wd_hbm, wd, 2)):
        pltpu.make_async_copy(src.at[0], dst, w_sem.at[s]).start()

    for k, (src, dst) in enumerate(((ql_hbm, ql_ref), (cl_hbm, cl_ref), (cr_hbm, cr_ref))):
        pltpu.make_async_copy(src, dst, in_sem.at[k]).start()

    xs[chip, c, :, pl.ds(0, D)] = normed_ref[...]
    lane = lax.broadcasted_iota(jnp.int32, (R, EXTRA), 1)
    same = lax.broadcasted_iota(jnp.int32, (R, R), 0) == lax.broadcasted_iota(jnp.int32, (R, R), 1)

    def column(ref, k):
        row = jnp.broadcast_to(ref[k : k + 1, :].astype(F32), (R, R))
        return jnp.sum(jnp.where(same, row, 0.0), axis=1, keepdims=True)

    tail = jnp.zeros((R, EXTRA), F32)
    for k in range(top):
        tail = jnp.where(lane == k, column(ids_ref, k), tail)
        tail = jnp.where(lane == top + k, column(lev_ref, k), tail)
    xs[chip, c, :, pl.ds(D, EXTRA)] = tail.astype(BF)

    pl.semaphore_wait(barrier, Z - 1 + (3 if planar else 1))

    pa = ag_rs.shape[1]
    wa = (D + EXTRA) // pa

    def ag(i, p, way, dev):
        part = xs.at[i, c, :, pl.ds(p * wa, wa)]
        return pltpu.make_async_remote_copy(
            part, part, ag_ss.at[way, i, p], ag_rs.at[i, p], device_id={"expert": dev}
        )

    def ag_core(i, cc):
        return pltpu.make_async_remote_copy(
            xs.at[i, cc], xs.at[i, cc], agc_ss.at[i], agc_rs.at[i], device_id={"expert": peer_c}
        )

    def got(i, p):
        ag(i, p, SIDE_A, peer_a).wait_recv()

    def ag_z(zz, p, way, dev):
        i = at(zz, a, b)
        part = xs.at[i, c, :, pl.ds(p * wa, wa)]
        return pltpu.make_async_remote_copy(
            part, part, agz_ss.at[way, zz, p], ag_rs.at[i, p], device_id={"expert": dev}
        )

    def go_up(zz, p):
        pl.when(z < Z - 1)(lambda: ag_z(zz, p, 0, me + 2 * plane).start())

    def go_down(zz, p):
        pl.when(z > 0)(lambda: ag_z(zz, p, 1, me - 2 * plane).start())

    def share(zz, wait, *onward):
        i = at(zz, a, b)
        for p in range(pa):
            if wait:
                got(i, p)
            for step in onward:
                step(zz, p)
            if planar:
                ag(i, p, SIDE_A, peer_a).start()
                ag(i, p, SIDE_B, peer_b).start()
        ag_core(i, c).start()

    def column_dev(zz):
        return me + 2 * plane * (zz - z)

    share(z, False, go_up, go_down)

    qr = qr_ref[...].astype(F32)
    heads, rope = ql_ref.shape[1], cr_ref.shape[1]
    for h in range(heads):
        rq[h * R : (h + 1) * R, :rope] = qr[:, h * rope : (h + 1) * rope]

    lmax = cl_ref.shape[1]
    for k, (src, dst) in enumerate(((ql_hbm, ql_ref), (cl_hbm, cl_ref), (cr_hbm, cr_ref))):
        pltpu.make_async_copy(src, dst, in_sem.at[k]).wait()

    def attend(t):
        keys = cl_ref[t]
        rope_q = rq[pl.ds(t, heads, stride=R), :rope].astype(BF)
        s = lax.dot_general(ql_ref[t], keys, (((1,), (1,)), ((), ())), preferred_element_type=F32)
        s = s + jnp.dot(rope_q, cr_ref[t], preferred_element_type=F32)
        s = s * score_scale
        seen = lax.broadcasted_iota(jnp.int32, (heads, lmax), 1) < len_ref[t]
        s = jnp.where(seen, s, -1e30)
        e = jnp.where(seen, jnp.exp(s - jnp.max(s, axis=-1, keepdims=True)), 0.0)
        p = (e / jnp.sum(e, axis=-1, keepdims=True)).astype(BF)
        att_ref[t] = jnp.dot(p, keys, preferred_element_type=F32).astype(BF)

    def from_a(zz):
        i = at(zz, 1 - a, b)
        for p in range(pa):
            got(i, p)
            ag(i, p, SIDE_B, peer_b).start()
        ag_core(i, c).start()

    if planar:
        from_a(z)

    def z_step(d, carry):
        pl.when(z - d >= 0)(lambda: share(z - d, True, go_up))
        pl.when(z + d < Z)(lambda: share(z + d, True, go_down))
        if planar:
            pl.when(z - d >= 0)(lambda: from_a(z - d))
            pl.when(z + d < Z)(lambda: from_a(z + d))
        return carry

    lax.fori_loop(1, Z, z_step, 0)

    if planar:
        def from_b(k, carry):
            attend(k)
            i = at((z + k // 2) % Z, k % 2, 1 - b)
            for p in range(pa):
                got(i, p)
            ag_core(i, c).start()
            return carry

        lax.fori_loop(0, 2 * Z, from_b, 0)
        first = min(2 * Z, R)
    else:
        first = 0
    for t in range(first, R):
        attend(t)

    pltpu.make_async_copy(att_ref, att_hbm, out_sem).start()

    def from_core(i, carry):
        ag_core(i, 1 - c).wait_recv()
        return carry

    lax.fori_loop(0, chips, from_core, 0)

    for src, dst, s in ((wg_hbm, wg, 0), (wu_hbm, wu, 1), (wd_hbm, wd, 2)):
        pltpu.make_async_copy(src.at[0], dst, w_sem.at[s]).wait()
    rows = n * R
    kc = 3584
    gacc[...] = jnp.zeros_like(gacc)
    uacc[...] = jnp.zeros_like(uacc)

    def k_step(k, carry):
        ks = pl.ds(pl.multiple_of(k * kc, kc), kc)
        xk = xs[:, :, :, ks].astype(F32).reshape(rows, kc).astype(BF)
        gacc[...] += jnp.dot(xk, wg[ks, :], preferred_element_type=F32)
        uacc[...] += jnp.dot(xk, wu[ks, :], preferred_element_type=F32)
        return carry

    lax.fori_loop(0, D // kc, k_step, 0)
    g = gacc[...]
    hidden = (g / (1.0 + jnp.exp(-g)) * uacc[...]).astype(BF)
    h3[...] = hidden.astype(F32).reshape(chips, 2, R, F)

    mine = place_ref[me].astype(F32)
    info = xs[:, :, :, pl.ds(D, EXTRA)].astype(F32).reshape(rows, EXTRA)
    levels = [info[:, top + k : top + k + 1] for k in range(top)]
    total = functools.reduce(lambda p, q: p + q, levels)
    coef = jnp.zeros((rows, 1), F32)
    for k in range(top):
        coef = coef + jnp.where(info[:, k : k + 1] == mine, route_scale * levels[k] / total, 0.0)
    cf[...] = jnp.broadcast_to(coef, (rows, EXTRA)).reshape(chips, 2, R, EXTRA)

    nc = 1792

    def down_half(cc):
        hh = h3[:, cc].reshape(chips * R, F).astype(BF)
        scale = cf[:, cc].reshape(chips * R, EXTRA)[:, :1]

        def n_step(k, carry):
            ns = pl.ds(pl.multiple_of(k * nc, nc), nc)
            p = jnp.dot(hh, wd[:, ns], preferred_element_type=F32).astype(BF).astype(F32)
            acc[:, cc, :, ns] = (p * scale).reshape(chips, R, nc).astype(BF)
            return carry

        lax.fori_loop(0, D // nc, n_step, 0)

    pr = rz_s.shape[1]
    wr = D // pr

    def cols(p):
        return pl.ds(p * wr, wr)

    def to_core(i):
        return pltpu.make_async_remote_copy(
            acc.at[i, 1 - c], rc.at[i], rsc_ss.at[i], rc_s.at[i], device_id={"expert": peer_c}
        )

    def to_b(zz, aa, p):
        i = at(zz, aa, 1 - b)
        return pltpu.make_async_remote_copy(
            acc.at[i, c, :, cols(p)], rb.at[zz, aa, :, cols(p)], rs_ss.at[SIDE_B, i, p],
            rb_s.at[zz, aa, p], device_id={"expert": peer_b},
        )

    def to_a(zz, p):
        i = at(zz, 1 - a, b)
        return pltpu.make_async_remote_copy(
            acc.at[i, c, :, cols(p)], ra.at[zz, :, cols(p)], rs_ss.at[SIDE_A, i, p],
            ra_s.at[zz, p], device_id={"expert": peer_a},
        )

    def to_z(zz, p):
        return pltpu.make_async_remote_copy(
            acc.at[at(zz, a, b), c, :, cols(p)], rz.at[z, :, cols(p)], rsz_ss.at[zz, p],
            rz_s.at[z, p], device_id={"expert": column_dev(zz)},
        )

    def from_z(zz, p):
        return pltpu.make_async_remote_copy(
            acc.at[chip, c, :, cols(p)], rz.at[zz, :, cols(p)], rsz_ss.at[zz, p],
            rz_s.at[zz, p], device_id={"expert": column_dev(zz)},
        )

    down_half(1 - c)

    def far(k):
        return (z + 1 + k) % Z

    def core_send(k, carry):
        if planar:
            q = k % (chips // 2)
            zz, other = far(q // 2), 1 - q % 2
            away = 1 - k // (chips // 2)
            aa = (1 - 2 * a) * away + a
            bb = (1 - 2 * b) * other + b
            to_core(at(zz, aa, bb)).start()
        else:
            to_core(far(k)).start()
        return carry

    lax.fori_loop(0, chips, core_send, 0)
    down_half(c)

    def plus(*terms):
        return functools.reduce(lambda p, q: p + q, [t.astype(F32) for t in terms])

    if planar:
        def b_send(k, carry):
            zz = far(k // 2)
            aa = (1 - 2 * a) * (1 - k % 2) + a
            i = at(zz, aa, 1 - b)
            to_core(i).wait_recv()
            acc[i, c] = plus(acc[i, c], rc[i]).astype(BF)
            for p in range(pr):
                to_b(zz, aa, p).start()
            return carry

        lax.fori_loop(0, 2 * Z, b_send, 0)

        def a_send(k):
            zz = far(k)
            i = at(zz, 1 - a, b)
            to_core(i).wait_recv()
            for p in range(pr):
                to_b(zz, 1 - a, p).wait_recv()
                cp = cols(p)
                acc[i, c, :, cp] = plus(acc[i, c, :, cp], rc[i, :, cp], rb[zz, 1 - a, :, cp]).astype(BF)
                to_a(zz, p).start()

        a_send(0)

    def column_sum(zz, p):
        i = at(zz, a, b)
        cp = cols(p)
        if planar:
            to_b(zz, a, p).wait_recv()
            to_a(zz, p).wait_recv()
            return plus(acc[i, c, :, cp], rc[i, :, cp], rb[zz, a, :, cp], ra[zz, :, cp])
        return plus(acc[i, c, :, cp], rc[i, :, cp])

    def z_send(k, carry):
        if planar:
            a_send(k + 1)
        zz = far(k)
        to_core(at(zz, a, b)).wait_recv()
        for p in range(pr):
            acc[at(zz, a, b), c, :, cols(p)] = column_sum(zz, p).astype(BF)
            to_z(zz, p).start()
        return carry

    lax.fori_loop(0, Z - 1, z_send, 0)
    to_core(chip).wait_recv()
    for p in range(pr):
        result = column_sum(z, p)
        for d in range(1, Z):
            zz = (z + d) % Z
            from_z(zz, p).wait_recv()
            result = result + rz[zz, :, cols(p)].astype(F32)
        moe_ref[:, cols(p)] = result.astype(BF)

    pltpu.make_async_copy(att_ref, att_hbm, out_sem).wait()

    def core_done(i, carry):
        ag_core(i, c).wait_send()
        to_core(i).wait_send()
        return carry

    lax.fori_loop(0, chips, core_done, 0)

    def z_done(zz, carry):
        i = at(zz, a, b)

        @pl.when(zz != z)
        def _():
            for p in range(pr):
                to_z(zz, p).wait_send()

        for p in range(pa):
            pl.when((zz <= z) & (z < Z - 1))(lambda: ag_z(zz, p, 0, me + 2 * plane).wait_send())
            pl.when((zz >= z) & (z > 0))(lambda: ag_z(zz, p, 1, me - 2 * plane).wait_send())
        if planar:
            for p in range(pa):
                ag(i, p, SIDE_A, peer_a).wait_send()
                for aa in range(2):
                    ag(at(zz, aa, b), p, SIDE_B, peer_b).wait_send()
            for p in range(pr):
                to_a(zz, p).wait_send()
                for aa in range(2):
                    to_b(zz, aa, p).wait_send()
        return carry

    lax.fori_loop(0, Z, z_done, 0)


def on_line(
    normed, expert_ids, gate_levels, placement, w_gate, w_up, w_down,
    q_latent, q_rope, cache_latent, cache_rope, lengths,
):
    n = lax.axis_size("expert")
    Z, Y, X = chip_grid(n)
    chips = n // 2
    R, D = normed.shape
    F = w_gate.shape[2]
    heads = q_latent.shape[1]
    vmem = pl.BlockSpec(memory_space=pltpu.VMEM)
    smem = pl.BlockSpec(memory_space=pltpu.SMEM)
    hbm = pl.BlockSpec(memory_space=pl.ANY)
    dma = pltpu.SemaphoreType.DMA
    side = Z if Y * X > 1 else 1
    pa, pr = parts(D + EXTRA, PA), parts(D, PR)
    return pl.pallas_call(
        functools.partial(line_body, n),
        out_shape=(
            jax.ShapeDtypeStruct((R, D), BF),
            jax.ShapeDtypeStruct(q_latent.shape, BF),
        ),
        in_specs=[vmem, vmem, vmem, smem, smem, hbm, hbm, hbm, hbm, vmem, hbm, hbm],
        out_specs=(vmem, hbm),
        scratch_shapes=[
            pltpu.VMEM((chips, 2, R, D + EXTRA), BF),
            pltpu.VMEM((chips, 2, R, D), BF),
            pltpu.VMEM((chips, R, D), BF),
            pltpu.VMEM((side, 2, R, D), BF),
            pltpu.VMEM((side, R, D), BF),
            pltpu.VMEM((Z, R, D), BF),
            pltpu.VMEM((D, F), BF),
            pltpu.VMEM((D, F), BF),
            pltpu.VMEM((F, D), BF),
            pltpu.VMEM((chips, 2, R, F), F32),
            pltpu.VMEM((chips, 2, R, EXTRA), F32),
            pltpu.VMEM((heads * R, 128), F32),
            pltpu.VMEM((n * R, F), F32),
            pltpu.VMEM((n * R, F), F32),
            pltpu.VMEM(q_latent.shape, BF),
            pltpu.VMEM(cache_latent.shape, BF),
            pltpu.VMEM(cache_rope.shape, BF),
            pltpu.VMEM(q_latent.shape, BF),
            dma((3,)),
            dma((3,)),
            dma,
            dma((2, chips, pa)),
            dma((chips, pa)),
            dma((2, Z, pa)),
            dma((chips,)),
            dma((chips,)),
            dma((2, chips, pr)),
            dma((Z, pr)),
            dma((chips,)),
            dma((chips,)),
            dma((side, 2, pr)),
            dma((side, pr)),
            dma((Z, pr)),
        ],
        compiler_params=pltpu.CompilerParams(
            collective_id=0, has_side_effects=True, vmem_limit_bytes=60 << 20
        ),
        cost_estimate=pl.CostEstimate(flops=3 * 10**9, bytes_accessed=13 * 10**6, transcendentals=300000),
    )(
        normed, expert_ids.T, gate_levels.T, lengths, placement, w_gate, w_up, w_down,
        q_latent, q_rope, cache_latent, cache_rope,
    )


def grid_body(
    n,
    normed_hbm, ids_hbm, lev_hbm, len_hbm, place_hbm, wg_hbm, wu_hbm, wd_hbm,
    ql_hbm, qr_hbm, cl_hbm, cr_hbm,
    moe_ref, att_ref,
    xs, acc, rc, r1, r2, r3, rf, wg, wu, wd, own, ids, lev, qr, rq, ql, cl, cr, lens, place,
    in_sem, w_sem,
    ag_ss, agc_ss, agf_ss, ag_rs, agc_rs, rs_ss, rs_rs, far_ss, far_rs,
):
    Z, Y, X = chip_grid(n)
    plane = Y * X
    R, D = own.shape
    W = D + EXTRA
    F = wg.shape[1]
    top = ids.shape[0]
    me = lax.axis_index("expert")
    c = me % 2
    chip = me // 2
    z = chip // plane
    y = (chip % plane) // X
    x = chip % X
    pair = z // 2
    here = (z % 2, y, x)
    steps = (2 * plane, 2 * X, 2)
    peers = [me + s * (1 - 2 * v) for s, v in zip(steps, here)]
    peer_c = 2 * chip + 1 - c
    peer_f = me + 2 * plane * ((z + 2) % Z - z)

    def group(q):
        return (pair + q) % 2

    def order(p):
        return tuple((1 + p + k) % 3 for k in range(3))

    def spot(flips):
        return tuple(1 - v if e in flips else v for e, v in enumerate(here))

    barrier = pltpu.get_barrier_semaphore()
    for dev in (peer_c, *peers, peer_f):
        pl.semaphore_signal(barrier, inc=1, device_id={"expert": dev})

    loads = [
        pltpu.make_async_copy(src, dst, in_sem.at[k])
        for k, (src, dst) in enumerate((
            (normed_hbm, own), (ids_hbm, ids), (lev_hbm, lev), (len_hbm, lens), (place_hbm, place),
            (qr_hbm, qr), (ql_hbm, ql), (cl_hbm, cl), (cr_hbm, cr),
        ))
    ]
    for load in loads:
        load.start()
    weights = [
        pltpu.make_async_copy(src.at[0], dst, w_sem.at[k])
        for k, (src, dst) in enumerate(((wg_hbm, wg), (wu_hbm, wu), (wd_hbm, wd)))
    ]
    for load in weights:
        load.start()
    for load in loads[:3]:
        load.wait()

    base = (c, pair, *here, slice(None))
    xs[(*base, pl.ds(0, D))] = own[...]
    lane = lax.broadcasted_iota(jnp.int32, (R, EXTRA), 1)
    same = lax.broadcasted_iota(jnp.int32, (R, R), 0) == lax.broadcasted_iota(jnp.int32, (R, R), 1)

    def column(ref, k):
        row = jnp.broadcast_to(ref[k : k + 1, :].astype(F32), (R, R))
        return jnp.sum(jnp.where(same, row, 0.0), axis=1, keepdims=True)

    tail = jnp.zeros((R, EXTRA), F32)
    for k in range(top):
        tail = jnp.where(lane == k, column(ids, k), tail)
        tail = jnp.where(lane == top + k, column(lev, k), tail)
    xs[(*base, pl.ds(D, EXTRA))] = tail.astype(BF)

    pl.semaphore_wait(barrier, 5)

    wa = W // 3

    def piece(p):
        return pl.ds(p * wa, wa)

    def gather(q, p, flips, level):
        e = order(p)[level]
        j = spot(flips)
        part = xs.at[(c, group(q), *j, slice(None), piece(p))]
        return pltpu.make_async_remote_copy(
            part, part, ag_ss.at[q, p, level], ag_rs.at[(q, *j, p)], device_id={"expert": peers[e]}
        )

    def last(p, flips):
        return max(order(p).index(e) for e in flips)

    def got(q, p, flips):
        gather(q, p, flips, 0).wait_recv()

    def to_far_block(p):
        part = xs.at[(*base, piece(p))]
        return pltpu.make_async_remote_copy(
            part, part, agf_ss, ag_rs.at[(1, *here, p)], device_id={"expert": peer_f}
        )

    def core_block(q, j, cc):
        part = xs.at[(cc, group(q), *j)]
        return pltpu.make_async_remote_copy(
            part, part, agc_ss, agc_rs.at[(q, *j)], device_id={"expert": peer_c}
        )

    def subsets(level):
        return [tuple(k for k in range(level) if m >> k & 1) + (level,) for m in range(1 << level)]

    def own_along(q, level):
        for p in range(3):
            gather(q, p, (), level).start()

    def stage(q, level):
        for p in range(3):
            for ks in subsets(level):
                flips = tuple(order(p)[k] for k in ks)
                got(q, p, flips)
                for later in range(level + 1, 3):
                    gather(q, p, flips, later).start()

    def cross(q):
        for flips in ((0,), (1,), (2,), (0, 1), (0, 2), (1, 2), (0, 1, 2)):
            for p in range(3):
                if last(p, flips) == 2:
                    got(q, p, flips)
            core_block(q, spot(flips), c).start()

    def own_core(q):
        core_block(q, here, c).start()

    def far_in():
        for p in range(3):
            got(1, p, ())

    def gathered(q):
        for m in range(8):
            core_block(q, (m // 4, m // 2 % 2, m % 2), 1 - c).wait_recv()

    def far_out():
        for p in range(3):
            to_far_block(p).start()

    def prepare():
        for load in loads[3:]:
            load.wait()
        queries = qr[...].astype(F32)
        for h in range(heads):
            rq[h * R : (h + 1) * R, :rope] = queries[:, h * rope : (h + 1) * rope]

    heads, rope = ql.shape[1], cr.shape[1]
    lmax = cl.shape[1]

    def attend(t):
        keys = cl[t]
        rope_q = rq[pl.ds(t, heads, stride=R), :rope].astype(BF)
        s = lax.dot_general(ql[t], keys, (((1,), (1,)), ((), ())), preferred_element_type=F32)
        s = s + jnp.dot(rope_q, cr[t], preferred_element_type=F32)
        s = s * score_scale
        seen = lax.broadcasted_iota(jnp.int32, (heads, lmax), 1) < lens[t]
        s = jnp.where(seen, s, -1e30)
        e = jnp.where(seen, jnp.exp(s - jnp.max(s, axis=-1, keepdims=True)), 0.0)
        p = (e / jnp.sum(e, axis=-1, keepdims=True)).astype(BF)
        att_ref[t] = jnp.dot(p, keys, preferred_element_type=F32).astype(BF)

    rows = 16 * R
    tiles = D // 128
    ends = [128 * (tiles * k // 3) for k in range(4)]

    def cols(p):
        return pl.ds(ends[p], ends[p + 1] - ends[p])

    def part_of(fixed):
        return tuple(fixed.get(e, slice(None)) for e in range(3))

    def scatter_order(p):
        return tuple((p + k) % 3 for k in range(3))

    def kept(p, level, flip):
        axes = scatter_order(p)
        fixed = {e: here[e] for e in axes[:level]}
        if level < 3:
            fixed[axes[level]] = 1 - here[axes[level]] if flip else here[axes[level]]
        return fixed

    landing = (r1, r2, r3)

    def to_core(q, p):
        g = group(q)
        return pltpu.make_async_remote_copy(
            acc.at[1 - c, g, :, :, :, :, cols(p)], rc.at[g, :, :, :, :, cols(p)],
            rs_ss.at[q, p, 3], rs_rs.at[q, p, 3], device_id={"expert": peer_c},
        )

    def scatter(q, p, level):
        g = group(q)
        e = scatter_order(p)[level]
        src = acc.at[(c, g, *part_of(kept(p, level, True)), slice(None), cols(p))]
        dst = landing[level].at[(g,) + (slice(None),) * (2 - level) + (slice(None), cols(p))]
        return pltpu.make_async_remote_copy(
            src, dst, rs_ss.at[q, p, level], rs_rs.at[q, p, level], device_id={"expert": peers[e]}
        )

    def to_far(p):
        return pltpu.make_async_remote_copy(
            acc.at[(c, group(1), *here, slice(None), cols(p))], rf.at[:, cols(p)],
            far_ss.at[p], far_rs.at[p], device_id={"expert": peer_f},
        )

    def total_of(q, p, fixed, levels):
        g, cp = group(q), cols(p)
        axes = scatter_order(p)
        j = part_of(fixed)
        terms = [acc[(c, g, *j, slice(None), cp)], rc[(g, *j, slice(None), cp)]]
        for level in range(levels):
            rest = [e for e in range(3) if e not in axes[: level + 1]]
            terms.append(landing[level][(g, *(j[e] for e in rest), slice(None), cp)])
        return functools.reduce(lambda u, v: u + v, [t.astype(F32) for t in terms])

    def send(q, p, level):
        (to_core(q, p) if level == 0 else scatter(q, p, level - 1)).wait_recv()
        fixed = kept(p, level, True)
        acc[(c, group(q), *part_of(fixed), slice(None), cols(p))] = total_of(q, p, fixed, level).astype(BF)
        scatter(q, p, level).start()

    def send_far(p):
        scatter(1, p, 2).wait_recv()
        acc[(c, group(1), *here, slice(None), cols(p))] = total_of(1, p, kept(p, 3, False), 3).astype(BF)
        to_far(p).start()

    def finish(p):
        scatter(0, p, 2).wait_recv()
        to_far(p).wait_recv()
        moe_ref[:, cols(p)] = (total_of(0, p, kept(p, 3, False), 3) + rf[:, cols(p)].astype(F32)).astype(BF)

    kc = D // 2

    def compute(q):
        gq = group(q)
        g = jnp.zeros((rows, F), F32)
        u = jnp.zeros((rows, F), F32)
        for k in range(D // kc):
            ks = pl.ds(k * kc, kc)
            xk = xs[:, gq, :, :, :, :, ks].astype(F32).reshape(rows, kc).astype(BF)
            g += jnp.dot(xk, wg[ks, :], preferred_element_type=F32)
            u += jnp.dot(xk, wu[ks, :], preferred_element_type=F32)
        hidden = (g / (1.0 + jnp.exp(-g)) * u).astype(BF)
        mine = place[me].astype(F32)
        info = xs[:, gq, :, :, :, :, pl.ds(D, EXTRA)].astype(F32).reshape(rows, EXTRA)
        levels = [info[:, top + k : top + k + 1] for k in range(top)]
        total = functools.reduce(lambda p, q: p + q, levels)
        coef = jnp.zeros((rows, 1), F32)
        for k in range(top):
            coef = coef + jnp.where(info[:, k : k + 1] == mine, route_scale * levels[k] / total, 0.0)
        for p in range(3):
            width = ends[p + 1] - ends[p]
            out = jnp.dot(hidden, wd[:, cols(p)], preferred_element_type=F32).astype(BF).astype(F32)
            acc[:, gq, :, :, :, :, cols(p)] = (out * coef).reshape(2, 2, 2, 2, R, width).astype(BF)
            to_core(q, p).start()

    def weights_in():
        for load in weights:
            load.wait()

    def sends(q, level):
        for p in range(3):
            send(q, p, level)

    own_along(0, 0)
    far_out()
    own_along(0, 1)
    own_along(0, 2)
    own_core(0)
    prepare()
    attend(0)
    attend(1)
    attend(2)
    stage(0, 0)
    far_in()
    own_along(1, 0)
    stage(0, 1)
    own_along(1, 1)
    own_core(1)
    attend(3)
    attend(4)
    cross(0)
    own_along(1, 2)
    attend(5)
    stage(1, 0)
    attend(6)
    weights_in()
    gathered(0)
    compute(0)
    stage(1, 1)
    attend(7)
    sends(0, 0)
    cross(1)
    gathered(1)
    compute(1)
    sends(1, 0)
    sends(1, 1)
    sends(0, 1)
    sends(1, 2)
    sends(0, 2)
    for p in range(3):
        send_far(p)
    for p in range(3):
        finish(p)

    for q in range(2):
        for p in range(3):
            one = xs.at[c, 0, 0, 0, 0, :, piece(p)]
            two = xs.at[c, 0, 0, 0, :, :, piece(p)]
            four = xs.at[c, 0, 0, :, :, :, piece(p)]
            for level, part in enumerate((one, two, four)):
                pltpu.make_async_copy(part, part, ag_ss.at[q, p, level]).wait()
    pltpu.make_async_copy(xs.at[base], xs.at[base], agf_ss).wait()
    pltpu.make_async_copy(xs.at[c], xs.at[c], agc_ss).wait()
    for p in range(3):
        for q in range(2):
            to_core(q, p).wait_send()
            for level in range(3):
                scatter(q, p, level).wait_send()
        to_far(p).wait_send()


def on_grid(
    normed, expert_ids, gate_levels, placement, w_gate, w_up, w_down,
    q_latent, q_rope, cache_latent, cache_rope, lengths,
):
    n = lax.axis_size("expert")
    R, D = normed.shape
    F = w_gate.shape[2]
    heads, top = q_latent.shape[1], expert_ids.shape[1]
    vmem = pl.BlockSpec(memory_space=pltpu.VMEM)
    hbm = pl.BlockSpec(memory_space=pl.ANY)
    dma = pltpu.SemaphoreType.DMA
    return pl.pallas_call(
        functools.partial(grid_body, n),
        out_shape=(pltpu.VMEM((R, D), BF), pltpu.VMEM(q_latent.shape, BF)),
        in_specs=[hbm] * 12,
        out_specs=(vmem, vmem),
        scratch_shapes=[
            pltpu.VMEM((2, 2, 2, 2, 2, R, D + EXTRA), BF),
            pltpu.VMEM((2, 2, 2, 2, 2, R, D), BF),
            pltpu.VMEM((2, 2, 2, 2, R, D), BF),
            pltpu.VMEM((2, 2, 2, R, D), BF),
            pltpu.VMEM((2, 2, R, D), BF),
            pltpu.VMEM((2, R, D), BF),
            pltpu.VMEM((R, D), BF),
            pltpu.VMEM((D, F), BF),
            pltpu.VMEM((D, F), BF),
            pltpu.VMEM((F, D), BF),
            pltpu.VMEM((R, D), BF),
            pltpu.VMEM((top, R), jnp.int32),
            pltpu.VMEM((top, R), jnp.int32),
            pltpu.VMEM(q_rope.shape, BF),
            pltpu.VMEM((heads * R, 128), F32),
            pltpu.VMEM(q_latent.shape, BF),
            pltpu.VMEM(cache_latent.shape, BF),
            pltpu.VMEM(cache_rope.shape, BF),
            pltpu.SMEM((R,), jnp.int32),
            pltpu.SMEM((n,), jnp.int32),
            dma((9,)),
            dma((3,)),
            dma((2, 3, 3)),
            dma,
            dma,
            dma((2, 2, 2, 2, 3)),
            dma((2, 2, 2, 2)),
            dma((2, 3, 4)),
            dma((2, 3, 4)),
            dma((3,)),
            dma((3,)),
        ],
        compiler_params=pltpu.CompilerParams(
            collective_id=0, has_side_effects=True, vmem_limit_bytes=60 << 20
        ),
        cost_estimate=pl.CostEstimate(flops=3 * 10**9, bytes_accessed=13 * 10**6, transcendentals=300000),
    )(
        normed, expert_ids.T, gate_levels.T, lengths, placement, w_gate, w_up, w_down,
        q_latent, q_rope, cache_latent, cache_rope,
    )


def per_device(*args):
    n = lax.axis_size("expert")
    Z, Y, X = chip_grid(n)
    return on_grid(*args) if Y * X > 1 else on_line(*args)


def solution(mesh):
    rows = ("groups", "expert")
    in_specs = (
        P(rows, None), P(rows, None), P(rows, None), P(),
        P("expert", None, None), P("expert", None, None), P("expert", None, None),
        P(rows, None, None), P(rows, None), P(rows, None, None), P(rows, None, None), P(rows),
    )
    out_specs = (P(rows, None), P(rows, None, None))
    return jax.shard_map(
        per_device, mesh=mesh, in_specs=in_specs, out_specs=out_specs, check_vma=False
    )
```
